128 devices in a mesh: dp: 128 (over x, z, y, core).
Axes of the slice: x: 4, y: 4, z: 4, core: 2. Of those that a mesh axis runs over, the one named last changes fastest.
Arguments:
- partials: bfloat16 [128, 256, 16384], P('dp'), may hold values from -96 to 96
- master: float32 [256, 16384], P('dp'), may hold values from -3 to 3
- moment_one: float32 [256, 16384], P('dp'), may hold values from -2 to 2
- moment_two: float32 [256, 16384], P('dp'), may hold values from 0.01 to 1
Outputs:
- master_new: float32 [256, 16384], P('dp')
- moment_one_new: float32 [256, 16384], P('dp')
- moment_two_new: float32 [256, 16384], P('dp')
- reduced_grad: float32 [256, 16384], P('dp')
- weights: bfloat16 [256, 16384], replicated
The draws below stay inside these ranges and needn't reach their ends.
All inputs are finite; a program needn't handle non-finite values. Where the reference program divides by a largest or mean magnitude, that divisor is 1e-20 or more.
Results may differ from the reference program's by a relative error of at most 0.012.
Values may be sent and summed in bfloat16 or wider, within the bound.
No kernel may reach another device: no remote copies, remote signals or barrier semaphores. Data moves between devices by JAX's collectives and lax.ppermute only.
A program may use at most 128 MiB of HBM per device.

```python
import math
import jax
import jax.numpy as jnp
from jax import lax

W = 16384
BLOCK = 128
MBITS = 7
STEP = 20
ROWS = 256
N_DP = 128


def with_spikes(values, rng, source, target, parts, factor):
    owner, partner = [(jnp.arange(values.shape[dim]) // (values.shape[dim] // parts)).reshape([-1 if axis == dim else 1 for axis in range(values.ndim)]) for dim in (source, target)]
    chosen = jax.random.permutation(rng, parts)[partner]
    strong = (owner == chosen) | (owner == (partner + parts // 2) % parts)
    return jnp.where(strong, factor * values, values)


def levels(key, dims, split, smallest, high):
    loudness = 1.0
    for axis_at, shards_of in split:
        steps = jax.random.uniform(jax.random.fold_in(jax.random.fold_in(key, 6), axis_at), (shards_of,), jnp.float32, smallest / len(split), high / len(split))
        loudness = loudness * jnp.repeat(jnp.exp(steps), dims[axis_at] // shards_of).reshape((-1,) + (1,) * (len(dims) - 1 - axis_at))
    return loudness


def scatter_about(stream_key, shape, width, bound, split=(), dtype=jnp.bfloat16):
    level = levels(stream_key, shape, split, -0.22, 0.18) if split else 1.0
    array = jax.random.normal(stream_key, shape, jnp.float32) * width * level
    return jnp.minimum(jnp.maximum(array, -bound), bound).astype(dtype)


def noise_with(key, extent, width, most, pieces, heavy, dtype=jnp.bfloat16):
    values = width * jax.random.normal(key, extent, jnp.float32)
    if pieces:
        values = values * levels(key, extent, pieces, -0.22, 0.18)
    return jnp.clip(with_spikes(values, jax.random.fold_in(key, 3), *heavy), -most, most).astype(dtype)


def setup_inputs(seed: int = 0) -> dict:
    arg_keys = jax.random.split(jax.random.key(seed), 5)
    return {
        "partials": noise_with(arg_keys[0], (N_DP, ROWS, W), 4.0, 96.0, ((0, 128),), (0, 1, 128, 5.5)),
        "master": scatter_about(arg_keys[1], (ROWS, W), 0.5, 3.0, ((0, 128),), jnp.float32),
        "moment_one": scatter_about(arg_keys[2], (ROWS, W), 0.3, 2.0, ((0, 128),), jnp.float32),
        "moment_two": jnp.clip(jnp.exp(math.log(1.0) - 4.6051702 * jax.random.uniform(arg_keys[3], (ROWS, W), jnp.float32) ** levels(arg_keys[3], (ROWS, W), ((0, 128),), -0.2, 0.2)), 0.01, 1.0),
    }


def block_scale(amax):
    powers = jnp.asarray([2.0 ** k for k in range(-20, 13)], jnp.float32)
    doubled = jnp.asarray([2.0 ** (k + 1) for k in range(-20, 13)], jnp.float32)
    inverse = jnp.asarray([2.0 ** (MBITS - k - 1) for k in range(-20, 13)], jnp.float32)
    hit = amax[..., None] >= powers
    scale = lax.optimization_barrier(jnp.max(jnp.where(hit, doubled, jnp.float32(2.0 ** (-20))), axis=-1))
    mult = lax.optimization_barrier(jnp.min(jnp.where(hit, inverse, jnp.float32(2.0 ** (MBITS + 20))), axis=-1))
    return (scale, mult)

def reference(partials, master, moment_one, moment_two):
    nblk = W // BLOCK

    def max_step(carry, piece):
        mags = jnp.abs(piece.astype(jnp.float32)).reshape(ROWS, nblk, BLOCK)
        return (jnp.maximum(carry, lax.optimization_barrier(jnp.max(mags, axis=2))), None)
    amax, _ = lax.scan(max_step, jnp.zeros((ROWS, nblk), jnp.float32), partials)
    scale, mult = block_scale(amax)

    def sum_step(carry, piece):
        vals = piece.astype(jnp.float32).reshape(ROWS, nblk, BLOCK) * mult[:, :, None]
        mant = jnp.floor(vals + 0.5)
        return (carry + mant, None)
    total, _ = lax.scan(sum_step, jnp.zeros((ROWS, nblk, BLOCK), jnp.float32), partials)
    factor = scale / (2.0 ** MBITS * N_DP)
    reduced_grad = (total * factor[:, :, None]).reshape(ROWS, W)
    moment_one_new = 0.9 * moment_one + 0.1 * reduced_grad
    moment_two_new = 0.95 * moment_two + 0.05 * reduced_grad * reduced_grad
    first = moment_one_new / (1.0 - 0.9 ** STEP)
    second = moment_two_new / (1.0 - 0.95 ** STEP)
    update = first / (jnp.sqrt(second) + 1e-08)
    master_new = master - 0.001 * (update + 0.1 * master)
    blocks = master_new.reshape(ROWS, nblk, BLOCK)
    wscale = lax.optimization_barrier(jnp.max(jnp.abs(blocks), axis=2)) + 1e-06
    wmant = (blocks / wscale[:, :, None]).astype(jnp.bfloat16)
    weights = (wmant.astype(jnp.float32) * wscale[:, :, None]).reshape(ROWS, W).astype(jnp.bfloat16)
    return (master_new, moment_one_new, moment_two_new, reduced_grad, weights)
```

```python
import jax
import jax.numpy as jnp
from jax import lax
from jax.experimental import pallas as pl
from jax.experimental.pallas import tpu as pltpu
from jax.sharding import PartitionSpec as P

BLOCK = 128
MBITS = 7
STEP = 20
ROWS = 256
W = 16384
N_DP = 128
HALF = W // 2
NB = HALF // BLOCK
F32 = jnp.float32
BF16 = jnp.bfloat16

NEAR = {0: ((0, 1), (3, 2)), 1: ((1, 2), (0, 3))}
FAR = {0: ((0, 3), (1, 2)), 1: ((0, 1), (2, 3))}
PLACE = {0: (0, 2, 3, 1), 1: (0, 1, 2, 3)}


def device(x, z, y, core):
    return ((x * 4 + z) * 4 + y) * 2 + core


def groups(pairs):
    return [
        [device(x, z, y, core) for x in px for z in pz for y in py]
        for core in (0, 1)
        for px in pairs[core]
        for pz in pairs[core]
        for py in pairs[core]
    ]


NEAR_GROUPS = groups(NEAR)
FAR_GROUPS = groups(FAR)
SWAP = [(d, d ^ 1) for d in range(N_DP)]


def exchange(x, among):
    return lax.all_to_all(x, "dp", 0, 0, axis_index_groups=among)


def spread(x, among):
    return exchange(jnp.broadcast_to(x[None], (8, *x.shape)), among)


def max_kernel(core_ref, x_ref, amax_ref, send_ref):
    rows = x_ref.shape[1]
    lane = lax.broadcasted_iota(jnp.int32, (rows, 128), 1)
    acc = jnp.zeros((rows, 128), F32)
    for b in range(W // BLOCK):
        v = jnp.abs(x_ref[0, :, b * BLOCK : (b + 1) * BLOCK].astype(F32))
        acc = jnp.where(lane == b, jnp.max(v, axis=1, keepdims=True), acc)
    amax_ref[...] = acc.astype(BF16)
    start = pl.multiple_of((1 - core_ref[0]) * HALF, HALF)
    send_ref[...] = x_ref[0, :, pl.ds(start, HALF)]


def block_max(core, partials, rows=32):
    return pl.pallas_call(
        max_kernel,
        out_shape=(
            jax.ShapeDtypeStruct((ROWS, 128), BF16),
            jax.ShapeDtypeStruct((ROWS, HALF), BF16),
        ),
        grid_spec=pltpu.PrefetchScalarGridSpec(
            num_scalar_prefetch=1,
            grid=(ROWS // rows,),
            in_specs=[pl.BlockSpec((1, rows, W), lambda i, c: (0, i, 0))],
            out_specs=[
                pl.BlockSpec((rows, 128), lambda i, c: (i, 0)),
                pl.BlockSpec((rows, HALF), lambda i, c: (i, 0)),
            ],
        ),
        name="block_max",
    )(core, partials)


def scale_of(amax):
    scale = jnp.full(amax.shape, 2.0**-20, F32)
    for k in range(-20, 13):
        scale = jnp.where(amax >= 2.0**k, F32(2.0 ** (k + 1)), scale)
    return scale


def mult_of(amax):
    mult = jnp.full(amax.shape, 2.0 ** (MBITS + 20), F32)
    for k in range(-20, 13):
        mult = jnp.where(amax >= 2.0**k, F32(2.0 ** (MBITS - k - 1)), mult)
    return mult


def quant_kernel(core_ref, place_ref, own_ref, other_ref, amax_ref, out_ref):
    core = core_ref[0]
    mult = mult_of(jnp.max(amax_ref[...].astype(F32), axis=0))
    mult = jnp.where(core == 0, mult, pltpu.roll(mult, 64, 1))
    top = lax.broadcasted_iota(jnp.int32, (8, 128), 0) < 4
    for b in range(NB):
        cols = slice(b * BLOCK, (b + 1) * BLOCK)
        m = jnp.broadcast_to(mult[:, b : b + 1], (16, BLOCK))
        v = jnp.floor(own_ref[0, :, cols].astype(F32) * m + 0.5)
        v = v + jnp.floor(other_ref[:, cols].astype(F32) * m + 0.5)
        t0, t1 = v[:8], v[8:]
        a = jnp.where(core == 1, t0, jnp.where(top, t0, t1))
        c = jnp.where(core == 1, t1, pltpu.roll(jnp.where(top, t1, t0), 4, 0))
        out_ref[0, 0, 0, 0, 0, :, cols] = a.astype(BF16)
        out_ref[0, 0, 1, 0, 0, :, cols] = c.astype(BF16)


def placed(x, z, place):
    px, pz = place[x], place[z]
    return (px >> 1, pz >> 1, 0, px & 1, pz & 1, 0, 0)


def quantise(core, place, partials, other, amax):
    out = pl.pallas_call(
        quant_kernel,
        out_shape=jax.ShapeDtypeStruct((2, 2, 2, 2, 2, 8, HALF), BF16),
        grid_spec=pltpu.PrefetchScalarGridSpec(
            num_scalar_prefetch=2,
            grid=(4, 4),
            in_specs=[
                pl.BlockSpec((1, 16, HALF), lambda x, z, c, p: (0, x * 4 + z, c[0])),
                pl.BlockSpec((16, HALF), lambda x, z, c, p: (x * 4 + z, 0)),
                pl.BlockSpec((8, 16, 128), lambda x, z, c, p: (0, x * 4 + z, 0)),
            ],
            out_specs=pl.BlockSpec(
                (1, 1, 2, 1, 1, 8, HALF), lambda x, z, c, p: placed(x, z, p)
            ),
        ),
        name="quantise",
    )(core, place, partials, other, amax)
    return out.reshape(8, 32, HALF)


def rows_kernel(core_ref, place_ref, w_ref, *refs):
    out_ref = refs[-1]
    core = core_ref[0]
    top = lax.broadcasted_iota(jnp.int32, (8, 128), 0) < 4
    for b in range(NB):
        cols = slice(b * BLOCK, (b + 1) * BLOCK)
        a = w_ref[0, 0, 0, 0, 0, :, cols].astype(F32)
        c = w_ref[0, 0, 1, 0, 0, :, cols].astype(F32)
        r = pltpu.roll(c, 4, 0)
        out_ref[:8, cols] = jnp.where(core == 1, a, jnp.where(top, a, r)).astype(BF16)
        out_ref[8:, cols] = jnp.where(core == 1, c, jnp.where(top, r, a)).astype(BF16)


def place_rows(core, place, w, before=None):
    w = w.reshape(2, 2, 2, 2, 2, 8, HALF)
    more = () if before is None else (before,)
    return pl.pallas_call(
        rows_kernel,
        out_shape=jax.ShapeDtypeStruct((ROWS, W), BF16),
        grid_spec=pltpu.PrefetchScalarGridSpec(
            num_scalar_prefetch=2,
            grid=(4, 4),
            in_specs=[
                pl.BlockSpec((1, 1, 2, 1, 1, 8, HALF), lambda x, z, c, p: placed(x, z, p)),
                *(pl.BlockSpec(memory_space=pl.ANY) for _ in more),
            ],
            out_specs=pl.BlockSpec((16, HALF), lambda x, z, c, p: (x * 4 + z, c[0])),
        ),
        input_output_aliases={3: 0} if more else {},
        name="place_rows",
    )(core, place, w, *more)


def per_device(partials, master, moment_one, moment_two):
    d = lax.axis_index("dp")
    core, chip = d % 2, d // 2
    places = jnp.asarray([PLACE[0], PLACE[1]], jnp.int32)
    mine = (core.reshape(1), places[core])
    theirs = ((1 - core).reshape(1), places[1 - core])

    amax, send = block_max(mine[0], partials)
    other = lax.ppermute(send, "dp", SWAP)
    amax = jnp.maximum(amax, lax.ppermute(amax, "dp", SWAP))
    amax = jnp.max(spread(amax, FAR_GROUPS), axis=0)
    amax = spread(amax, NEAR_GROUPS)

    state = jnp.stack([master, moment_one, moment_two])
    state_own = lax.dynamic_slice_in_dim(state, core * HALF, HALF, 2)
    state_other = lax.ppermute(
        lax.dynamic_slice_in_dim(state, (1 - core) * HALF, HALF, 2), "dp", SWAP
    )
    first = core == 0
    state = jnp.where(
        first,
        jnp.concatenate([state_own, state_other], axis=1),
        jnp.concatenate([state_other, state_own], axis=1),
    )
    master, moment_one, moment_two = state

    mant = quantise(*mine, partials, other, amax)
    mant = jnp.sum(exchange(mant, NEAR_GROUPS).astype(F32), axis=0).reshape(8, 4, HALF)
    total = jnp.sum(exchange(mant, FAR_GROUPS), axis=0)

    own_amax = lax.dynamic_slice(amax, (0, chip * 4, core * NB), (8, 4, NB))
    scale = scale_of(jnp.max(own_amax.astype(F32), axis=0))
    factor = scale / (2.0**MBITS * N_DP)
    reduced_grad = (total.reshape(4, NB, BLOCK) * factor[:, :, None]).reshape(4, HALF)
    moment_one_new = 0.9 * moment_one + 0.1 * reduced_grad
    moment_two_new = 0.95 * moment_two + 0.05 * reduced_grad * reduced_grad
    update = (moment_one_new / (1.0 - 0.9**STEP)) / (
        jnp.sqrt(moment_two_new / (1.0 - 0.95**STEP)) + 1e-08
    )
    master_new = master - 0.001 * (update + 0.1 * master)
    blocks = master_new.reshape(4, NB, BLOCK)
    wscale = jnp.max(jnp.abs(blocks), axis=2) + 1e-06
    wmant = (blocks / wscale[:, :, None]).astype(BF16)
    weights = (wmant.astype(F32) * wscale[:, :, None]).reshape(4, HALF).astype(BF16)

    out = jnp.stack([master_new, moment_one_new, moment_two_new, reduced_grad])
    out_own = jnp.where(first, out[:, :2], out[:, 2:])
    out_other = lax.ppermute(jnp.where(first, out[:, 2:], out[:, :2]), "dp", SWAP)
    out = jnp.where(
        first,
        jnp.concatenate([out_own, out_other], axis=2),
        jnp.concatenate([out_other, out_own], axis=2),
    )

    weights = spread(weights, FAR_GROUPS).reshape(32, HALF)
    weights = spread(weights, NEAR_GROUPS)
    weights_other = lax.ppermute(weights, "dp", SWAP)
    full = place_rows(*mine, weights)
    full = place_rows(*theirs, weights_other, full)
    return (out[0], out[1], out[2], out[3], full)


def solution(mesh):
    in_specs = (P("dp", None, None), P("dp", None), P("dp", None), P("dp", None))
    out_specs = (P("dp", None), P("dp", None), P("dp", None), P("dp", None), P())
    return jax.shard_map(
        per_device, mesh=mesh, in_specs=in_specs, out_specs=out_specs, check_vma=False
    )
```

```python
import jax
import jax.numpy as jnp
from jax import lax
from jax.experimental import pallas as pl
from jax.experimental.pallas import tpu as pltpu
from jax.sharding import PartitionSpec as P

BLOCK = 128
MBITS = 7
STEP = 20
ROWS = 256
W = 16384
N_DP = 128
HALF = W // 2
NB = HALF // BLOCK
F32 = jnp.float32
BF16 = jnp.bfloat16

F16 = jnp.float16

NEAR = {0: ((0, 1), (3, 2)), 1: ((1, 2), (0, 3))}
FAR = {0: ((0, 3), (1, 2)), 1: ((0, 1), (2, 3))}
OWNER = {0: (0, 2, 3, 1), 1: (0, 1, 2, 3)}
ALL = [(x, z, y) for x in range(4) for z in range(4) for y in range(4)]


def device(x, z, y, core):
    return ((x * 4 + z) * 4 + y) * 2 + core


def groups(pairs):
    return [
        [device(x, z, y, core) for x in px for z in pz for y in py]
        for core in (0, 1)
        for px in pairs[core]
        for pz in pairs[core]
        for py in pairs[core]
    ]


def owner(core, at):
    return tuple(OWNER[core][i] for i in at)


NEAR_GROUPS = groups(NEAR)
FAR_GROUPS = groups(FAR)
SWAP = [(d, d ^ 1) for d in range(N_DP)]
TO_SAME = [(device(*owner(c, at), c), device(*at, c)) for c in (0, 1) for at in ALL]
TO_OTHER = [(device(*owner(c, at), 1 - c), device(*at, c)) for c in (0, 1) for at in ALL]
FROM_SAME = [(b, a) for a, b in TO_SAME]
FROM_OTHER = [(b, a) for a, b in TO_OTHER]


def exchange(x, among):
    return lax.all_to_all(x, "dp", 0, 0, axis_index_groups=among)


def spread(x, among):
    return exchange(jnp.broadcast_to(x[None], (8, *x.shape)), among)


def max_kernel(core_ref, x_ref, amax_ref, other_ref, send_ref, buf, own_max, other_max, in_sem, out_sem):
    core = core_ref[0]
    rows = ROWS // in_sem.shape[0]
    theirs = pl.ds(pl.multiple_of((1 - core) * HALF, HALF), HALF)
    chunks = [pl.ds(i * rows, rows) for i in range(ROWS // rows)]
    loads = [
        pltpu.make_async_copy(x_ref.at[0, at], buf.at[at], in_sem.at[i])
        for i, at in enumerate(chunks)
    ]
    stores = [
        pltpu.make_async_copy(buf.at[at, theirs], send_ref.at[at], out_sem.at[i])
        for i, at in enumerate(chunks)
    ]
    for load in loads:
        load.start()
    lane = lax.broadcasted_iota(jnp.int32, (rows, 128), 1)
    low = lane < NB
    for i, at in enumerate(chunks):
        loads[i].wait()
        stores[i].start()
        acc = jnp.zeros((rows, 128), F32)
        for b in range(W // BLOCK):
            v = jnp.abs(buf[at, b * BLOCK : (b + 1) * BLOCK].astype(F32))
            acc = jnp.where(lane == b, jnp.max(v, axis=1, keepdims=True), acc)
        rolled = pltpu.roll(acc, NB, 1)
        mine, rest = jnp.where(core == 0, acc, rolled), jnp.where(core == 0, rolled, acc)
        to = pl.ds(i * rows % 128, rows)
        if i * rows < 128:
            own_max[to, :], other_max[to, :] = mine, rest
        else:
            own_max[to, :] = jnp.where(low, own_max[to, :], rest)
            other_max[to, :] = jnp.where(low, other_max[to, :], mine)
    amax_ref[...] = own_max[...].astype(BF16)
    other_ref[...] = other_max[...].astype(BF16)
    for store in stores:
        store.wait()


SMEM = pl.BlockSpec(memory_space=pltpu.SMEM)
VMEM = pl.BlockSpec(memory_space=pltpu.VMEM)
HBM = pl.BlockSpec(memory_space=pltpu.HBM)
PARAMS = pltpu.CompilerParams(vmem_limit_bytes=60 << 20)


def block_max(core, partials, chunks=4):
    return pl.pallas_call(
        max_kernel,
        out_shape=(
            jax.ShapeDtypeStruct((128, 128), BF16),
            jax.ShapeDtypeStruct((128, 128), BF16),
            jax.ShapeDtypeStruct((ROWS, HALF), BF16),
        ),
        in_specs=[SMEM, HBM],
        out_specs=[VMEM, VMEM, HBM],
        scratch_shapes=[
            pltpu.VMEM((ROWS, W), BF16),
            pltpu.VMEM((128, 128), F32),
            pltpu.VMEM((128, 128), F32),
            pltpu.SemaphoreType.DMA((chunks,)),
            pltpu.SemaphoreType.DMA((chunks,)),
        ],
        compiler_params=PARAMS,
        name="block_max",
    )(core, partials)


def scale_of(amax):
    scale = jnp.full(amax.shape, 2.0**-20, F32)
    for k in range(-20, 13):
        scale = jnp.where(amax >= 2.0**k, F32(2.0 ** (k + 1)), scale)
    return scale


def mult_of(amax):
    mult = jnp.full(amax.shape, 2.0 ** (MBITS + 20), F32)
    for k in range(-20, 13):
        mult = jnp.where(amax >= 2.0**k, F32(2.0 ** (MBITS - k - 1)), mult)
    return mult


def quant_kernel(core_ref, x_ref, other_ref, amax_ref, out_ref, own, other, mant, own_sem, other_sem, out_sem):
    rows = ROWS // own_sem.shape[0]
    mine = pl.ds(pl.multiple_of(core_ref[0] * HALF, HALF), HALF)
    loads = []
    for i in range(ROWS // rows):
        at = pl.ds(i * rows, rows)
        loads.append(
            (
                pltpu.make_async_copy(x_ref.at[0, at, mine], own.at[at], own_sem.at[i]),
                pltpu.make_async_copy(other_ref.at[at], other.at[at], other_sem.at[i]),
            )
        )
        for load in loads[i]:
            load.start()
    stores = []
    for i in range(ROWS // rows):
        at = pl.ds(i * rows, rows)
        low = i * rows % 128
        mult = mult_of(jnp.max(amax_ref[:, low : low + rows, :].astype(F32), axis=0))
        for load in loads[i]:
            load.wait()
        for b in range(NB):
            cols = slice(b * BLOCK, (b + 1) * BLOCK)
            lane = b + (NB if i * rows >= 128 else 0)
            m = jnp.broadcast_to(mult[:, lane : lane + 1], (rows, BLOCK))
            v = jnp.floor(own[at, cols].astype(F32) * m + 0.5)
            v = v + jnp.floor(other[at, cols].astype(F32) * m + 0.5)
            mant[at, cols] = v.astype(BF16)
        for t in range(i * rows // 8, (i + 1) * rows // 8):
            x, z, y = t // 8, t // 2 % 4, t % 2
            stores.append(
                pltpu.make_async_copy(
                    mant.at[pl.ds(t * 8, 8)],
                    out_ref.at[x >> 1, z >> 1, y, x & 1, z & 1],
                    out_sem.at[t],
                )
            )
            stores[t].start()
    for store in stores:
        store.wait()


def quantise(core, partials, other, amax, chunks=8):
    out = pl.pallas_call(
        quant_kernel,
        out_shape=jax.ShapeDtypeStruct((2, 2, 2, 2, 2, 8, HALF), BF16),
        in_specs=[SMEM, HBM, HBM, VMEM],
        out_specs=HBM,
        scratch_shapes=[
            *[pltpu.VMEM((ROWS, HALF), BF16)] * 3,
            pltpu.SemaphoreType.DMA((chunks,)),
            pltpu.SemaphoreType.DMA((chunks,)),
            pltpu.SemaphoreType.DMA((ROWS // 8,)),
        ],
        compiler_params=PARAMS,
        name="quantise",
    )(core, partials, other, amax)
    return out.reshape(8, 32, HALF)


def rows_kernel(half_ref, w_ref, *refs):
    out_ref, buf, in_sem, out_sem = refs[-4:]
    half = pl.ds(pl.multiple_of(half_ref[0] * HALF, HALF), HALF)
    loads, stores = [], []
    for t in range(ROWS // 8):
        x, z, y = t // 8, t // 2 % 4, t % 2
        source = w_ref.at[x >> 1, z >> 1, y, x & 1, z & 1]
        loads.append(pltpu.make_async_copy(source, buf.at[t], in_sem.at[t]))
        target = out_ref.at[pl.ds(t * 8, 8), half]
        stores.append(pltpu.make_async_copy(buf.at[t], target, out_sem.at[t]))
    for load in loads:
        load.start()
    for load, store in zip(loads, stores):
        load.wait()
        store.start()
    for store in stores:
        store.wait()


def place_rows(half, w, before=None):
    more = () if before is None else (before,)
    return pl.pallas_call(
        rows_kernel,
        out_shape=jax.ShapeDtypeStruct((ROWS, W), BF16),
        in_specs=[SMEM, HBM, *(HBM for _ in more)],
        out_specs=HBM,
        scratch_shapes=[
            pltpu.VMEM((ROWS // 8, 8, HALF), BF16),
            pltpu.SemaphoreType.DMA((ROWS // 8,)),
            pltpu.SemaphoreType.DMA((ROWS // 8,)),
        ],
        input_output_aliases={2: 0} if more else {},
        compiler_params=PARAMS,
        name="place_rows",
    )(half, w.reshape(2, 2, 2, 2, 2, 8, HALF), *more)


def per_device(partials, master, moment_one, moment_two):
    d = lax.axis_index("dp")
    core = d & 1
    first = core == 0
    place = [jnp.where((i == 0) | ~first, i, jnp.where(i == 3, 1, i + 1)) for i in (d >> 5, (d >> 3) & 3, (d >> 1) & 3)]
    row = place[0] * 64 + place[1] * 16 + place[2] * 4

    amax, amax_send, send = block_max(core.reshape(1), partials)
    amax_other = lax.ppermute(amax_send, "dp", SWAP)
    send, amax_other = lax.optimization_barrier((send, amax_other))
    other = lax.ppermute(send, "dp", SWAP)
    amax = jnp.max(spread(jnp.maximum(amax, amax_other), FAR_GROUPS), axis=0)
    amax = spread(amax, NEAR_GROUPS)

    state = jnp.stack([master, moment_one, moment_two])
    state_same = lax.dynamic_slice_in_dim(state, core * HALF, HALF, 2)
    state_other = lax.dynamic_slice_in_dim(state, (1 - core) * HALF, HALF, 2)
    state_same = lax.ppermute(state_same, "dp", TO_SAME)
    state_other = lax.ppermute(state_other, "dp", TO_OTHER)
    state = jnp.where(
        first,
        jnp.concatenate([state_same, state_other], axis=1),
        jnp.concatenate([state_other, state_same], axis=1),
    )
    master, moment_one, moment_two = state

    mant = quantise(core.reshape(1), partials, other, amax)
    mant = jnp.sum(exchange(mant, NEAR_GROUPS).astype(F32), axis=0).astype(F16)
    total = jnp.sum(exchange(mant.reshape(8, 4, HALF), FAR_GROUPS).astype(F32), axis=0)

    own_amax = lax.dynamic_slice(amax, (0, row & 127, (row >> 7) * NB), (8, 4, NB))
    scale = scale_of(jnp.max(own_amax.astype(F32), axis=0))
    factor = scale / (2.0**MBITS * N_DP)
    reduced_grad = (total.reshape(4, NB, BLOCK) * factor[:, :, None]).reshape(4, HALF)
    moment_one_new = 0.9 * moment_one + 0.1 * reduced_grad
    moment_two_new = 0.95 * moment_two + 0.05 * reduced_grad * reduced_grad
    update = (moment_one_new / (1.0 - 0.9**STEP)) / (
        jnp.sqrt(moment_two_new / (1.0 - 0.95**STEP)) + 1e-08
    )
    master_new = master - 0.001 * (update + 0.1 * master)
    blocks = master_new.reshape(4, NB, BLOCK)
    wscale = jnp.max(jnp.abs(blocks), axis=2) + 1e-06
    wmant = (blocks / wscale[:, :, None]).astype(BF16)
    weights = (wmant.astype(F32) * wscale[:, :, None]).reshape(4, HALF).astype(BF16)

    out = jnp.stack([master_new, moment_one_new, moment_two_new, reduced_grad])
    out_same = lax.ppermute(jnp.where(first, out[:, :2], out[:, 2:]), "dp", FROM_SAME)
    out_other = lax.ppermute(jnp.where(first, out[:, 2:], out[:, :2]), "dp", FROM_OTHER)
    out = jnp.where(
        first,
        jnp.concatenate([out_same, out_other], axis=2),
        jnp.concatenate([out_other, out_same], axis=2),
    )

    weights = spread(weights, FAR_GROUPS).reshape(32, HALF)
    weights = spread(weights, NEAR_GROUPS)
    weights_other = lax.ppermute(weights, "dp", SWAP)
    full = place_rows(core.reshape(1), weights)
    full = place_rows((1 - core).reshape(1), weights_other, full)
    return (out[0], out[1], out[2], out[3], full)


def solution(mesh):
    in_specs = (P("dp", None, None), P("dp", None), P("dp", None), P("dp", None))
    out_specs = (P("dp", None), P("dp", None), P("dp", None), P("dp", None), P())
    return jax.shard_map(
        per_device, mesh=mesh, in_specs=in_specs, out_specs=out_specs, check_vma=False
    )
```

```python
import jax
import jax.numpy as jnp
from jax import lax
from jax.experimental import pallas as pl
from jax.experimental.pallas import tpu as pltpu
from jax.sharding import PartitionSpec as P

BLOCK = 128
MBITS = 7
STEP = 20
ROWS = 256
W = 16384
N_DP = 128
HALF = W // 2
NB = HALF // BLOCK
F32 = jnp.float32
BF16 = jnp.bfloat16

F16 = jnp.float16

NEAR = {0: ((0, 1), (2, 3)), 1: ((1, 2), (0, 3))}
FAR = {0: ((1, 2), (0, 3)), 1: ((0, 1), (2, 3))}
OWNER = {0: (0, 2, 3, 1), 1: (0, 1, 2, 3)}
ALL = [(x, z, y) for x in range(4) for z in range(4) for y in range(4)]


def device(x, z, y, core):
    return ((x * 4 + z) * 4 + y) * 2 + core


def groups(pairs):
    return [
        [device(x, z, y, core) for x in px for z in pz for y in py]
        for core in (0, 1)
        for px in pairs[core]
        for pz in pairs[core]
        for py in pairs[core]
    ]


def owner(core, at):
    return tuple(OWNER[core][i] for i in at)


NEAR_GROUPS = groups(NEAR)
FAR_GROUPS = groups(FAR)
SWAP = [(d, d ^ 1) for d in range(N_DP)]
TO_SAME = [(device(*owner(c, at), c), device(*at, c)) for c in (0, 1) for at in ALL]
TO_OTHER = [(device(*owner(c, at), 1 - c), device(*at, c)) for c in (0, 1) for at in ALL]
FROM_SAME = [(b, a) for a, b in TO_SAME]
FROM_OTHER = [(b, a) for a, b in TO_OTHER]


def exchange(x, among):
    return lax.all_to_all(x, "dp", 0, 0, axis_index_groups=among)


def spread(x, among):
    return exchange(jnp.broadcast_to(x[None], (8, *x.shape)), among)


def max_kernel(core_ref, x_ref, amax_ref, other_ref, send_ref, buf, own_max, other_max, in_sem, out_sem):
    core = core_ref[0]
    rows = ROWS // in_sem.shape[0]
    theirs = pl.ds(pl.multiple_of((1 - core) * HALF, HALF), HALF)
    chunks = [pl.ds(i * rows, rows) for i in range(ROWS // rows)]
    loads = [
        pltpu.make_async_copy(x_ref.at[0, at], buf.at[at], in_sem.at[i])
        for i, at in enumerate(chunks)
    ]
    stores = [
        pltpu.make_async_copy(buf.at[at, theirs], send_ref.at[at], out_sem.at[i])
        for i, at in enumerate(chunks)
    ]
    for load in loads:
        load.start()
    lane = lax.broadcasted_iota(jnp.int32, (rows, 128), 1)
    low = lane < NB
    for i, at in enumerate(chunks):
        loads[i].wait()
        stores[i].start()
        acc = jnp.zeros((rows, 128), F32)
        for b in range(W // BLOCK):
            v = jnp.abs(buf[at, b * BLOCK : (b + 1) * BLOCK].astype(F32))
            acc = jnp.where(lane == b, jnp.max(v, axis=1, keepdims=True), acc)
        rolled = pltpu.roll(acc, NB, 1)
        mine, rest = jnp.where(core == 0, acc, rolled), jnp.where(core == 0, rolled, acc)
        to = pl.ds(i * rows % 128, rows)
        if i * rows < 128:
            own_max[to, :], other_max[to, :] = mine, rest
        else:
            own_max[to, :] = jnp.where(low, own_max[to, :], rest)
            other_max[to, :] = jnp.where(low, other_max[to, :], mine)
    amax_ref[...] = own_max[...].astype(BF16)
    other_ref[...] = other_max[...].astype(BF16)
    for store in stores:
        store.wait()


SMEM = pl.BlockSpec(memory_space=pltpu.SMEM)
VMEM = pl.BlockSpec(memory_space=pltpu.VMEM)
HBM = pl.BlockSpec(memory_space=pltpu.HBM)
PARAMS = pltpu.CompilerParams(vmem_limit_bytes=60 << 20)


def block_max(core, partials, chunks=4):
    return pl.pallas_call(
        max_kernel,
        out_shape=(
            jax.ShapeDtypeStruct((128, 128), BF16),
            jax.ShapeDtypeStruct((128, 128), BF16),
            jax.ShapeDtypeStruct((ROWS, HALF), BF16),
        ),
        in_specs=[SMEM, HBM],
        out_specs=[VMEM, VMEM, HBM],
        scratch_shapes=[
            pltpu.VMEM((ROWS, W), BF16),
            pltpu.VMEM((128, 128), F32),
            pltpu.VMEM((128, 128), F32),
            pltpu.SemaphoreType.DMA((chunks,)),
            pltpu.SemaphoreType.DMA((chunks,)),
        ],
        compiler_params=PARAMS,
        name="block_max",
    )(core, partials)


def scale_of(amax):
    scale = jnp.full(amax.shape, 2.0**-20, F32)
    for k in range(-20, 13):
        scale = jnp.where(amax >= 2.0**k, F32(2.0 ** (k + 1)), scale)
    return scale


def mult_of(amax):
    mult = jnp.full(amax.shape, 2.0 ** (MBITS + 20), F32)
    for k in range(-20, 13):
        mult = jnp.where(amax >= 2.0**k, F32(2.0 ** (MBITS - k - 1)), mult)
    return mult


def flipped(at_ref, x, z, y):
    return ((x >> 1) ^ at_ref[1], (z >> 1) ^ at_ref[2], y ^ at_ref[3], x & 1, z & 1)


def quant_kernel(at_ref, x_ref, other_ref, amax_ref, out_ref, own, other, mant, own_sem, other_sem, out_sem):
    rows = ROWS // own_sem.shape[0]
    mine = pl.ds(pl.multiple_of(at_ref[0] * HALF, HALF), HALF)
    loads = []
    for i in range(ROWS // rows):
        at = pl.ds(i * rows, rows)
        loads.append(
            (
                pltpu.make_async_copy(x_ref.at[0, at, mine], own.at[at], own_sem.at[i]),
                pltpu.make_async_copy(other_ref.at[at], other.at[at], other_sem.at[i]),
            )
        )
        for load in loads[i]:
            load.start()
    stores = []
    for i in range(ROWS // rows):
        at = pl.ds(i * rows, rows)
        low = i * rows % 128
        mult = mult_of(jnp.max(amax_ref[:, low : low + rows, :].astype(F32), axis=0))
        for load in loads[i]:
            load.wait()
        for b in range(NB):
            cols = slice(b * BLOCK, (b + 1) * BLOCK)
            lane = b + (NB if i * rows >= 128 else 0)
            m = jnp.broadcast_to(mult[:, lane : lane + 1], (rows, BLOCK))
            v = jnp.floor(own[at, cols].astype(F32) * m + 0.5)
            v = v + jnp.floor(other[at, cols].astype(F32) * m + 0.5)
            mant[at, cols] = v.astype(BF16)
        for t in range(i * rows // 8, (i + 1) * rows // 8):
            x, z, y = t // 8, t // 2 % 4, t % 2
            stores.append(
                pltpu.make_async_copy(
                    mant.at[pl.ds(t * 8, 8)],
                    out_ref.at[flipped(at_ref, x, z, y)],
                    out_sem.at[t],
                )
            )
            stores[t].start()
    for store in stores:
        store.wait()


def quantise(at, partials, other, amax, chunks=8):
    out = pl.pallas_call(
        quant_kernel,
        out_shape=jax.ShapeDtypeStruct((2, 2, 2, 2, 2, 8, HALF), BF16),
        in_specs=[SMEM, HBM, HBM, VMEM],
        out_specs=HBM,
        scratch_shapes=[
            *[pltpu.VMEM((ROWS, HALF), BF16)] * 3,
            pltpu.SemaphoreType.DMA((chunks,)),
            pltpu.SemaphoreType.DMA((chunks,)),
            pltpu.SemaphoreType.DMA((ROWS // 8,)),
        ],
        compiler_params=PARAMS,
        name="quantise",
    )(at, partials, other, amax)
    return out.reshape(8, 32, HALF)


def rows_kernel(at_ref, w_ref, *refs):
    out_ref, buf, in_sem, out_sem = refs[-4:]
    half = pl.ds(pl.multiple_of(at_ref[0] * HALF, HALF), HALF)
    loads, stores = [], []
    for t in range(ROWS // 8):
        x, z, y = t // 8, t // 2 % 4, t % 2
        source = w_ref.at[flipped(at_ref, x, z, y)]
        loads.append(pltpu.make_async_copy(source, buf.at[t], in_sem.at[t]))
        target = out_ref.at[pl.ds(t * 8, 8), half]
        stores.append(pltpu.make_async_copy(buf.at[t], target, out_sem.at[t]))
    for load in loads:
        load.start()
    for load, store in zip(loads, stores):
        load.wait()
        store.start()
    for store in stores:
        store.wait()


def place_rows(at, w, before=None):
    more = () if before is None else (before,)
    return pl.pallas_call(
        rows_kernel,
        out_shape=jax.ShapeDtypeStruct((ROWS, W), BF16),
        in_specs=[SMEM, HBM, *(HBM for _ in more)],
        out_specs=HBM,
        scratch_shapes=[
            pltpu.VMEM((ROWS // 8, 8, HALF), BF16),
            pltpu.SemaphoreType.DMA((ROWS // 8,)),
            pltpu.SemaphoreType.DMA((ROWS // 8,)),
        ],
        input_output_aliases={2: 0} if more else {},
        compiler_params=PARAMS,
        name="place_rows",
    )(at, w.reshape(2, 2, 2, 2, 2, 8, HALF), *more)


def per_device(partials, master, moment_one, moment_two):
    d = lax.axis_index("dp")
    core = d & 1
    first = core == 0
    chip = (d >> 5, (d >> 3) & 3, (d >> 1) & 3)
    at = [jnp.stack([c, *((1 - c) * (i >> 1) for i in chip)]) for c in (core, 1 - core)]
    place = [jnp.where((i == 0) | ~first, i, jnp.where(i == 3, 1, i + 1)) for i in chip]
    row = place[0] * 64 + place[1] * 16 + place[2] * 4

    amax, amax_send, send = block_max(core.reshape(1), partials)
    amax_other = lax.ppermute(amax_send, "dp", SWAP)
    send, amax_other = lax.optimization_barrier((send, amax_other))
    other = lax.ppermute(send, "dp", SWAP)
    amax = jnp.max(spread(jnp.maximum(amax, amax_other), FAR_GROUPS), axis=0)
    amax = spread(amax, NEAR_GROUPS)

    state = jnp.stack([master, moment_one, moment_two])
    state_same = lax.dynamic_slice_in_dim(state, core * HALF, HALF, 2)
    state_other = lax.dynamic_slice_in_dim(state, (1 - core) * HALF, HALF, 2)
    state_same = lax.ppermute(state_same, "dp", TO_SAME)
    state_other = lax.ppermute(state_other, "dp", TO_OTHER)
    state = jnp.where(
        first,
        jnp.concatenate([state_same, state_other], axis=1),
        jnp.concatenate([state_other, state_same], axis=1),
    )
    master, moment_one, moment_two = state

    mant = quantise(at[0], partials, other, amax)
    mant = jnp.sum(exchange(mant, NEAR_GROUPS).astype(F32), axis=0).astype(F16)
    total = jnp.sum(exchange(mant.reshape(8, 4, HALF), FAR_GROUPS).astype(F32), axis=0)

    own_amax = lax.dynamic_slice(amax, (0, row & 127, (row >> 7) * NB), (8, 4, NB))
    scale = scale_of(jnp.max(own_amax.astype(F32), axis=0))
    factor = scale / (2.0**MBITS * N_DP)
    reduced_grad = (total.reshape(4, NB, BLOCK) * factor[:, :, None]).reshape(4, HALF)
    moment_one_new = 0.9 * moment_one + 0.1 * reduced_grad
    moment_two_new = 0.95 * moment_two + 0.05 * reduced_grad * reduced_grad
    update = (moment_one_new / (1.0 - 0.9**STEP)) / (
        jnp.sqrt(moment_two_new / (1.0 - 0.95**STEP)) + 1e-08
    )
    master_new = master - 0.001 * (update + 0.1 * master)
    blocks = master_new.reshape(4, NB, BLOCK)
    wscale = jnp.max(jnp.abs(blocks), axis=2) + 1e-06
    wmant = (blocks / wscale[:, :, None]).astype(BF16)
    weights = (wmant.astype(F32) * wscale[:, :, None]).reshape(4, HALF).astype(BF16)

    out = jnp.stack([master_new, moment_one_new, moment_two_new, reduced_grad])
    out_same = lax.ppermute(jnp.where(first, out[:, :2], out[:, 2:]), "dp", FROM_SAME)
    out_other = lax.ppermute(jnp.where(first, out[:, 2:], out[:, :2]), "dp", FROM_OTHER)
    out = jnp.where(
        first,
        jnp.concatenate([out_same, out_other], axis=2),
        jnp.concatenate([out_other, out_same], axis=2),
    )

    weights = spread(weights, FAR_GROUPS).reshape(32, HALF)
    weights = spread(weights, NEAR_GROUPS)
    weights_other = lax.ppermute(weights, "dp", SWAP)
    full = place_rows(at[0], weights)
    full = place_rows(at[1], weights_other, full)
    return (out[0], out[1], out[2], out[3], full)


def solution(mesh):
    in_specs = (P("dp", None, None), P("dp", None), P("dp", None), P("dp", None))
    out_specs = (P("dp", None), P("dp", None), P("dp", None), P("dp", None), P())
    return jax.shard_map(
        per_device, mesh=mesh, in_specs=in_specs, out_specs=out_specs, check_vma=False
    )
```

```python
import jax
import jax.numpy as jnp
from jax import lax
from jax.experimental import pallas as pl
from jax.experimental.pallas import tpu as pltpu
from jax.sharding import PartitionSpec as P

BLOCK = 128
MBITS = 7
STEP = 20
ROWS = 256
W = 16384
N_DP = 128
HALF = W // 2
NB = HALF // BLOCK
F32 = jnp.float32
BF16 = jnp.bfloat16
CHIPS = 64

PAIRS = (((0, 1), (2, 3)), ((1, 2), (0, 3)))


def device(x, z, y, core):
    return ((x * 4 + z) * 4 + y) * 2 + core


def groups(pairs):
    return [
        [device(x, z, y, core) for x in px for z in pz for y in py]
        for core in (0, 1)
        for px in pairs
        for pz in pairs
        for py in pairs
    ]


CUBES = [groups(pairs) for pairs in PAIRS]
SAME_CORE = [[2 * chip + core for chip in range(CHIPS)] for core in (0, 1)]
SWAP = [(d, d ^ 1) for d in range(N_DP)]


def exchange(x, among):
    return lax.all_to_all(x, "dp", 0, 0, axis_index_groups=among)


def spread(x, among):
    return exchange(jnp.broadcast_to(x[None], (len(among[0]), *x.shape)), among)


def max_kernel(core_ref, x_ref, amax_ref, other_ref, send_ref, buf, own_max, other_max, in_sem, out_sem):
    core = core_ref[0]
    rows = ROWS // in_sem.shape[0]
    theirs = pl.ds(pl.multiple_of((1 - core) * HALF, HALF), HALF)
    chunks = [pl.ds(i * rows, rows) for i in range(ROWS // rows)]
    loads = [
        pltpu.make_async_copy(x_ref.at[0, at], buf.at[at], in_sem.at[i])
        for i, at in enumerate(chunks)
    ]
    stores = [
        pltpu.make_async_copy(buf.at[at, theirs], send_ref.at[at], out_sem.at[i])
        for i, at in enumerate(chunks)
    ]
    for load in loads:
        load.start()
    lane = lax.broadcasted_iota(jnp.int32, (rows, 128), 1)
    low = lane < NB
    for i, at in enumerate(chunks):
        loads[i].wait()
        stores[i].start()
        acc = jnp.zeros((rows, 128), F32)
        for b in range(W // BLOCK):
            v = jnp.abs(buf[at, b * BLOCK : (b + 1) * BLOCK].astype(F32))
            acc = jnp.where(lane == b, jnp.max(v, axis=1, keepdims=True), acc)
        rolled = pltpu.roll(acc, NB, 1)
        mine, rest = jnp.where(core == 0, acc, rolled), jnp.where(core == 0, rolled, acc)
        to = pl.ds(i * rows % 128, rows)
        if i * rows < 128:
            own_max[to, :], other_max[to, :] = mine, rest
        else:
            own_max[to, :] = jnp.where(low, own_max[to, :], rest)
            other_max[to, :] = jnp.where(low, other_max[to, :], mine)
    amax_ref[...] = own_max[...].astype(BF16)
    other_ref[...] = other_max[...].astype(BF16)
    for store in stores:
        store.wait()


SMEM = pl.BlockSpec(memory_space=pltpu.SMEM)
VMEM = pl.BlockSpec(memory_space=pltpu.VMEM)
HBM = pl.BlockSpec(memory_space=pltpu.HBM)
PARAMS = pltpu.CompilerParams(vmem_limit_bytes=60 << 20)


def block_max(core, partials, chunks=4):
    return pl.pallas_call(
        max_kernel,
        out_shape=(
            jax.ShapeDtypeStruct((128, 128), BF16),
            jax.ShapeDtypeStruct((128, 128), BF16),
            jax.ShapeDtypeStruct((ROWS, HALF), BF16),
        ),
        in_specs=[SMEM, HBM],
        out_specs=[VMEM, VMEM, HBM],
        scratch_shapes=[
            pltpu.VMEM((ROWS, W), BF16),
            pltpu.VMEM((128, 128), F32),
            pltpu.VMEM((128, 128), F32),
            pltpu.SemaphoreType.DMA((chunks,)),
            pltpu.SemaphoreType.DMA((chunks,)),
        ],
        compiler_params=PARAMS,
        name="block_max",
    )(core, partials)


def scale_of(amax):
    scale = jnp.full(amax.shape, 2.0**-20, F32)
    for k in range(-20, 13):
        scale = jnp.where(amax >= 2.0**k, F32(2.0 ** (k + 1)), scale)
    return scale


def mult_of(amax):
    mult = jnp.full(amax.shape, 2.0 ** (MBITS + 20), F32)
    for k in range(-20, 13):
        mult = jnp.where(amax >= 2.0**k, F32(2.0 ** (MBITS - k - 1)), mult)
    return mult


PART = HALF // 2


def top_rows():
    return lax.broadcasted_iota(jnp.int32, (8, BLOCK), 0) < 4


def quant_kernel(core_ref, x_ref, other_ref, amax_ref, out_ref, own, other, mant, own_sem, other_sem, out_sem):
    chunks = own_sem.shape[0]
    rows = ROWS // chunks
    mine = pl.ds(pl.multiple_of(core_ref[0] * HALF, HALF), HALF)
    loads, stores = [], []
    for i in range(chunks):
        at = pl.ds(i * rows, rows)
        loads.append(
            (
                pltpu.make_async_copy(x_ref.at[0, at, mine], own.at[at], own_sem.at[i]),
                pltpu.make_async_copy(other_ref.at[at], other.at[at], other_sem.at[i]),
            )
        )
        for load in loads[i]:
            load.start()
    top = top_rows()
    for i in range(chunks):
        at = pl.ds(i * rows, rows)
        low = i * rows % 128
        mult = mult_of(jnp.max(amax_ref[:, low : low + rows, :].astype(F32), axis=0))

        def mantissas(b):
            cols = slice(b * BLOCK, (b + 1) * BLOCK)
            lane = b + (NB if i * rows >= 128 else 0)
            m = jnp.broadcast_to(mult[:, lane : lane + 1], (rows, BLOCK))
            v = jnp.floor(own[at, cols].astype(F32) * m + 0.5)
            return v + jnp.floor(other[at, cols].astype(F32) * m + 0.5)

        for load in loads[i]:
            load.wait()
        for b in range(NB // 2):
            left, right = mantissas(b), mantissas(b + NB // 2)
            cols = slice(b * BLOCK, (b + 1) * BLOCK)
            for t in range(rows // 8):
                l, r = left[t * 8 : t * 8 + 8], right[t * 8 : t * 8 + 8]
                chip = (i * rows // 8 + t) * 2
                mant[chip, :, cols] = jnp.where(top, l, pltpu.roll(r, 4, 0)).astype(BF16)
                mant[chip + 1, :, cols] = jnp.where(top, pltpu.roll(l, 4, 0), r).astype(BF16)
        at = pl.ds(i * rows // 4, rows // 4)
        stores.append(pltpu.make_async_copy(mant.at[at], out_ref.at[at], out_sem.at[i]))
        stores[i].start()
    for store in stores:
        store.wait()


def quantise(core, partials, other, amax, chunks=8):
    return pl.pallas_call(
        quant_kernel,
        out_shape=jax.ShapeDtypeStruct((CHIPS, 8, PART), BF16),
        in_specs=[SMEM, HBM, HBM, VMEM],
        out_specs=HBM,
        scratch_shapes=[
            pltpu.VMEM((ROWS, HALF), BF16),
            pltpu.VMEM((ROWS, HALF), BF16),
            pltpu.VMEM((CHIPS, 8, PART), BF16),
            pltpu.SemaphoreType.DMA((chunks,)),
            pltpu.SemaphoreType.DMA((chunks,)),
            pltpu.SemaphoreType.DMA((chunks,)),
        ],
        compiler_params=PARAMS,
        name="quantise",
    )(core, partials, other, amax)


def rows_kernel(half_ref, w_ref, *refs):
    out_ref, got, full, in_sem, out_sem = refs[-5:]
    chunks = in_sem.shape[0]
    rows = ROWS // chunks
    half = pl.ds(pl.multiple_of(half_ref[0] * HALF, HALF), HALF)
    loads, stores = [], []
    for i in range(chunks):
        at = pl.ds(i * rows // 4, rows // 4)
        loads.append(pltpu.make_async_copy(w_ref.at[at], got.at[at], in_sem.at[i]))
        at = pl.ds(i * rows, rows)
        stores.append(pltpu.make_async_copy(full.at[at], out_ref.at[at, half], out_sem.at[i]))
        loads[i].start()
    top = top_rows()
    for i in range(chunks):
        loads[i].wait()
        for t in range(i * rows // 8, (i + 1) * rows // 8):
            for b in range(NB // 2):
                cols = slice(b * BLOCK, (b + 1) * BLOCK)
                u = got[2 * t, :, cols].astype(F32)
                v = got[2 * t + 1, :, cols].astype(F32)
                full[t * 8 : t * 8 + 8, cols] = jnp.where(top, u, pltpu.roll(v, 4, 0)).astype(BF16)
                cols = slice(PART + b * BLOCK, PART + (b + 1) * BLOCK)
                full[t * 8 : t * 8 + 8, cols] = jnp.where(top, pltpu.roll(u, 4, 0), v).astype(BF16)
        stores[i].start()
    for store in stores:
        store.wait()


def place_rows(half, w, before=None, chunks=8):
    more = () if before is None else (before,)
    return pl.pallas_call(
        rows_kernel,
        out_shape=jax.ShapeDtypeStruct((ROWS, W), BF16),
        in_specs=[SMEM, HBM, *(HBM for _ in more)],
        out_specs=HBM,
        scratch_shapes=[
            pltpu.VMEM((CHIPS, 8, PART), BF16),
            pltpu.VMEM((ROWS, HALF), BF16),
            pltpu.SemaphoreType.DMA((chunks,)),
            pltpu.SemaphoreType.DMA((chunks,)),
        ],
        input_output_aliases={2: 0} if more else {},
        compiler_params=PARAMS,
        name="place_rows",
    )(half, w, *more)


def per_device(partials, master, moment_one, moment_two):
    d = lax.axis_index("dp")
    core, chip = d & 1, d >> 1
    first = core == 0
    row = chip * 4

    amax, amax_send, send = block_max(core.reshape(1), partials)
    amax_other = lax.ppermute(amax_send, "dp", SWAP)
    send, amax_other = lax.optimization_barrier((send, amax_other))
    other = lax.ppermute(send, "dp", SWAP)
    amax = jnp.max(spread(jnp.maximum(amax, amax_other), CUBES[0]), axis=0)
    amax = spread(amax, CUBES[1])

    state = jnp.stack([master, moment_one, moment_two])
    state_own = lax.dynamic_slice_in_dim(state, core * HALF, HALF, 2)
    state_other = lax.dynamic_slice_in_dim(state, (1 - core) * HALF, HALF, 2)
    state_other = lax.ppermute(state_other, "dp", SWAP)
    state = jnp.where(
        first,
        jnp.concatenate([state_own, state_other], axis=1),
        jnp.concatenate([state_other, state_own], axis=1),
    )
    master, moment_one, moment_two = state

    mant = exchange(quantise(core.reshape(1), partials, other, amax), SAME_CORE)
    total = jnp.sum(mant.astype(F32), axis=0)
    total = total.reshape(2, 4, PART).transpose(1, 0, 2).reshape(4, HALF)

    own_amax = lax.dynamic_slice(amax, (0, row & 127, (row >> 7) * NB), (8, 4, NB))
    scale = scale_of(jnp.max(own_amax.astype(F32), axis=0))
    factor = scale / (2.0**MBITS * N_DP)
    reduced_grad = (total.reshape(4, NB, BLOCK) * factor[:, :, None]).reshape(4, HALF)
    moment_one_new = 0.9 * moment_one + 0.1 * reduced_grad
    moment_two_new = 0.95 * moment_two + 0.05 * reduced_grad * reduced_grad
    update = (moment_one_new / (1.0 - 0.9**STEP)) / (
        jnp.sqrt(moment_two_new / (1.0 - 0.95**STEP)) + 1e-08
    )
    master_new = master - 0.001 * (update + 0.1 * master)
    blocks = master_new.reshape(4, NB, BLOCK)
    wscale = jnp.max(jnp.abs(blocks), axis=2) + 1e-06
    wmant = (blocks / wscale[:, :, None]).astype(BF16)
    weights = (wmant.astype(F32) * wscale[:, :, None]).reshape(4, HALF).astype(BF16)

    out = jnp.stack([master_new, moment_one_new, moment_two_new, reduced_grad])
    out_own = jnp.where(first, out[:, :2], out[:, 2:])
    out_other = lax.ppermute(jnp.where(first, out[:, 2:], out[:, :2]), "dp", SWAP)
    out = jnp.where(
        first,
        jnp.concatenate([out_own, out_other], axis=2),
        jnp.concatenate([out_other, out_own], axis=2),
    )

    weights = weights.reshape(4, 2, PART).transpose(1, 0, 2).reshape(8, PART)
    weights = spread(weights, SAME_CORE)
    weights_other = lax.ppermute(weights, "dp", SWAP)
    full = place_rows(core.reshape(1), weights)
    full = place_rows((1 - core).reshape(1), weights_other, full)
    return (out[0], out[1], out[2], out[3], full)


def solution(mesh):
    in_specs = (P("dp", None, None), P("dp", None), P("dp", None), P("dp", None))
    out_specs = (P("dp", None), P("dp", None), P("dp", None), P("dp", None), P())
    return jax.shard_map(
        per_device, mesh=mesh, in_specs=in_specs, out_specs=out_specs, check_vma=False
    )
```

```python
import jax
import jax.numpy as jnp
from jax import lax
from jax.experimental import pallas as pl
from jax.experimental.pallas import tpu as pltpu
from jax.sharding import PartitionSpec as P

BLOCK = 128
MBITS = 7
STEP = 20
ROWS = 256
W = 16384
N_DP = 128
HALF = W // 2
NB = HALF // BLOCK
F32 = jnp.float32
BF16 = jnp.bfloat16
F16 = jnp.float16

NEAR = {0: ((0, 1), (3, 2)), 1: ((1, 2), (0, 3))}
FAR = {0: ((0, 3), (1, 2)), 1: ((0, 1), (2, 3))}
PLACE = {0: (0, 2, 3, 1), 1: (0, 1, 2, 3)}
CUBES = ({0: FAR[1], 1: FAR[1]}, {0: NEAR[1], 1: NEAR[1]})


def device(x, z, y, core):
    return ((x * 4 + z) * 4 + y) * 2 + core


def groups(pairs):
    return [
        [device(x, z, y, core) for x in px for z in pz for y in py]
        for core in (0, 1)
        for px in pairs[core]
        for pz in pairs[core]
        for py in pairs[core]
    ]


NEAR_GROUPS = groups(NEAR)
FAR_GROUPS = groups(FAR)
SWAP = [(d, d ^ 1) for d in range(N_DP)]


def exchange(x, among):
    return lax.all_to_all(x, "dp", 0, 0, axis_index_groups=among)


def spread(x, among):
    return exchange(jnp.broadcast_to(x[None], (len(among[0]), *x.shape)), among)


def max_kernel(core_ref, x_ref, amax_ref, other_ref, send_ref, buf, own_max, other_max, in_sem, out_sem):
    core = core_ref[0]
    rows = ROWS // in_sem.shape[0]
    theirs = pl.ds(pl.multiple_of((1 - core) * HALF, HALF), HALF)
    chunks = [pl.ds(i * rows, rows) for i in range(ROWS // rows)]
    loads = [
        pltpu.make_async_copy(x_ref.at[0, at], buf.at[at], in_sem.at[i])
        for i, at in enumerate(chunks)
    ]
    stores = [
        pltpu.make_async_copy(buf.at[at, theirs], send_ref.at[at], out_sem.at[i])
        for i, at in enumerate(chunks)
    ]
    for load in loads:
        load.start()
    lane = lax.broadcasted_iota(jnp.int32, (rows, 128), 1)
    low = lane < NB
    for i, at in enumerate(chunks):
        loads[i].wait()
        stores[i].start()
        acc = jnp.zeros((rows, 128), F32)
        for b in range(W // BLOCK):
            v = jnp.abs(buf[at, b * BLOCK : (b + 1) * BLOCK].astype(F32))
            acc = jnp.where(lane == b, jnp.max(v, axis=1, keepdims=True), acc)
        rolled = pltpu.roll(acc, NB, 1)
        mine, rest = jnp.where(core == 0, acc, rolled), jnp.where(core == 0, rolled, acc)
        to = pl.ds(i * rows % 128, rows)
        if i * rows < 128:
            own_max[to, :], other_max[to, :] = mine, rest
        else:
            own_max[to, :] = jnp.where(low, own_max[to, :], rest)
            other_max[to, :] = jnp.where(low, other_max[to, :], mine)
    amax_ref[...] = own_max[...].astype(BF16)
    other_ref[...] = other_max[...].astype(BF16)
    for store in stores:
        store.wait()


SMEM = pl.BlockSpec(memory_space=pltpu.SMEM)
VMEM = pl.BlockSpec(memory_space=pltpu.VMEM)
HBM = pl.BlockSpec(memory_space=pltpu.HBM)
PARAMS = pltpu.CompilerParams(vmem_limit_bytes=60 << 20)


def block_max(core, partials, chunks=4):
    return pl.pallas_call(
        max_kernel,
        out_shape=(
            jax.ShapeDtypeStruct((128, 128), BF16),
            jax.ShapeDtypeStruct((128, 128), BF16),
            jax.ShapeDtypeStruct((ROWS, HALF), BF16),
        ),
        in_specs=[SMEM, HBM],
        out_specs=[VMEM, VMEM, HBM],
        scratch_shapes=[
            pltpu.VMEM((ROWS, W), BF16),
            pltpu.VMEM((128, 128), F32),
            pltpu.VMEM((128, 128), F32),
            pltpu.SemaphoreType.DMA((chunks,)),
            pltpu.SemaphoreType.DMA((chunks,)),
        ],
        compiler_params=PARAMS,
        name="block_max",
    )(core, partials)


def scale_of(amax):
    scale = jnp.full(amax.shape, 2.0**-20, F32)
    for k in range(-20, 13):
        scale = jnp.where(amax >= 2.0**k, F32(2.0 ** (k + 1)), scale)
    return scale


def mult_of(amax):
    mult = jnp.full(amax.shape, 2.0 ** (MBITS + 20), F32)
    for k in range(-20, 13):
        mult = jnp.where(amax >= 2.0**k, F32(2.0 ** (MBITS - k - 1)), mult)
    return mult


def block_of(at_ref, x, z, y):
    px, pz = at_ref[1 + x], at_ref[1 + z]
    return (px >> 1, pz >> 1, y, px & 1, pz & 1)


def tile_mask(at_ref):
    row = lax.broadcasted_iota(jnp.int32, (8, BLOCK), 0)
    return row < 4 + 4 * at_ref[0], 4 * (1 - at_ref[0])


def quant_kernel(at_ref, x_ref, other_ref, amax_ref, out_ref, own, other, mant, own_sem, other_sem, out_sem):
    chunks = own_sem.shape[0]
    rows = ROWS // chunks
    mine = pl.ds(pl.multiple_of(at_ref[0] * HALF, HALF), HALF)
    loads, stores = [], []
    for i in range(chunks):
        at = pl.ds(i * rows, rows)
        loads.append(
            (
                pltpu.make_async_copy(x_ref.at[0, at, mine], own.at[at], own_sem.at[i]),
                pltpu.make_async_copy(other_ref.at[at], other.at[at], other_sem.at[i]),
            )
        )
        for load in loads[i]:
            load.start()
    keep, turn = tile_mask(at_ref)
    for i in range(chunks):
        at = pl.ds(i * rows, rows)
        low = i * rows % 128
        mult = mult_of(jnp.max(amax_ref[:, low : low + rows, :].astype(F32), axis=0))
        for load in loads[i]:
            load.wait()
        for b in range(NB):
            cols = slice(b * BLOCK, (b + 1) * BLOCK)
            lane = b + (NB if i * rows >= 128 else 0)
            m = jnp.broadcast_to(mult[:, lane : lane + 1], (rows, BLOCK))
            v = jnp.floor(own[at, cols].astype(F32) * m + 0.5)
            v = v + jnp.floor(other[at, cols].astype(F32) * m + 0.5)
            for t in range(0, rows // 8, 2):
                p, q = v[t * 8 : t * 8 + 8], v[t * 8 + 8 : t * 8 + 16]
                tile = i * rows // 8 + t
                mant[tile, :, cols] = jnp.where(keep, p, q).astype(BF16)
                mant[tile + 1, :, cols] = pltpu.roll(jnp.where(keep, q, p), turn, 0).astype(BF16)
        for t in range(i * rows // 8, (i + 1) * rows // 8):
            target = out_ref.at[block_of(at_ref, t // 8, t // 2 % 4, t % 2)]
            stores.append(pltpu.make_async_copy(mant.at[t], target, out_sem.at[t]))
            stores[t].start()
    for store in stores:
        store.wait()


def quantise(at, partials, other, amax, chunks=8):
    out = pl.pallas_call(
        quant_kernel,
        out_shape=jax.ShapeDtypeStruct((2, 2, 2, 2, 2, 8, HALF), BF16),
        in_specs=[SMEM, HBM, HBM, VMEM],
        out_specs=HBM,
        scratch_shapes=[
            pltpu.VMEM((ROWS, HALF), BF16),
            pltpu.VMEM((ROWS, HALF), BF16),
            pltpu.VMEM((ROWS // 8, 8, HALF), BF16),
            pltpu.SemaphoreType.DMA((chunks,)),
            pltpu.SemaphoreType.DMA((chunks,)),
            pltpu.SemaphoreType.DMA((ROWS // 8,)),
        ],
        compiler_params=PARAMS,
        name="quantise",
    )(at, partials, other, amax)
    return out.reshape(8, 32, HALF)


def rows_kernel(at_ref, w_ref, *refs):
    out_ref, got, full, in_sem, out_sem = refs[-5:]
    chunks = out_sem.shape[0]
    rows = ROWS // chunks
    half = pl.ds(pl.multiple_of(at_ref[0] * HALF, HALF), HALF)
    loads, stores = [], []
    for t in range(ROWS // 8):
        source = w_ref.at[block_of(at_ref, t // 8, t // 2 % 4, t % 2)]
        loads.append(pltpu.make_async_copy(source, got.at[t], in_sem.at[t]))
        loads[t].start()
    for i in range(chunks):
        at = pl.ds(i * rows, rows)
        stores.append(pltpu.make_async_copy(full.at[at], out_ref.at[at, half], out_sem.at[i]))
    keep, turn = tile_mask(at_ref)
    for i in range(chunks):
        for t in range(i * rows // 8, (i + 1) * rows // 8, 2):
            loads[t].wait()
            loads[t + 1].wait()
            for b in range(NB):
                cols = slice(b * BLOCK, (b + 1) * BLOCK)
                p = got[t, :, cols].astype(F32)
                q = pltpu.roll(got[t + 1, :, cols].astype(F32), turn, 0)
                full[t * 8 : t * 8 + 8, cols] = jnp.where(keep, p, q).astype(BF16)
                full[t * 8 + 8 : t * 8 + 16, cols] = jnp.where(keep, q, p).astype(BF16)
        stores[i].start()
    for store in stores:
        store.wait()


def place_rows(at, w, before=None, chunks=8):
    more = () if before is None else (before,)
    return pl.pallas_call(
        rows_kernel,
        out_shape=jax.ShapeDtypeStruct((ROWS, W), BF16),
        in_specs=[SMEM, HBM, *(HBM for _ in more)],
        out_specs=HBM,
        scratch_shapes=[
            pltpu.VMEM((ROWS // 8, 8, HALF), BF16),
            pltpu.VMEM((ROWS, HALF), BF16),
            pltpu.SemaphoreType.DMA((ROWS // 8,)),
            pltpu.SemaphoreType.DMA((chunks,)),
        ],
        input_output_aliases={2: 0} if more else {},
        compiler_params=PARAMS,
        name="place_rows",
    )(at, w.reshape(2, 2, 2, 2, 2, 8, HALF), *more)


def per_device(partials, master, moment_one, moment_two):
    d = lax.axis_index("dp")
    core, chip = d & 1, d >> 1
    first = core == 0
    row = chip * 4
    places = [jnp.where(first, PLACE[0][i], PLACE[1][i]) for i in range(4)]
    others = [jnp.where(first, PLACE[1][i], PLACE[0][i]) for i in range(4)]
    mine, theirs = jnp.stack([core, *places]), jnp.stack([1 - core, *others])

    amax, amax_send, send = block_max(core.reshape(1), partials)
    amax_other = lax.ppermute(amax_send, "dp", SWAP)
    send, amax_other = lax.optimization_barrier((send, amax_other))
    other = lax.ppermute(send, "dp", SWAP)
    amax = jnp.max(spread(jnp.maximum(amax, amax_other), groups(CUBES[0])), axis=0)
    amax = spread(amax, groups(CUBES[1]))

    state = jnp.stack([master, moment_one, moment_two])
    state_own = lax.dynamic_slice_in_dim(state, core * HALF, HALF, 2)
    state_other = lax.dynamic_slice_in_dim(state, (1 - core) * HALF, HALF, 2)
    state_other = lax.ppermute(state_other, "dp", SWAP)
    state = jnp.where(
        first,
        jnp.concatenate([state_own, state_other], axis=1),
        jnp.concatenate([state_other, state_own], axis=1),
    )
    master, moment_one, moment_two = state

    mant = exchange(quantise(mine, partials, other, amax), NEAR_GROUPS)
    mant = jnp.sum(mant.astype(F32), axis=0).astype(F16).reshape(8, 4, HALF)
    total = jnp.sum(exchange(mant, FAR_GROUPS).astype(F32), axis=0)

    own_amax = lax.dynamic_slice(amax, (0, row & 127, (row >> 7) * NB), (8, 4, NB))
    scale = scale_of(jnp.max(own_amax.astype(F32), axis=0))
    factor = scale / (2.0**MBITS * N_DP)
    reduced_grad = (total.reshape(4, NB, BLOCK) * factor[:, :, None]).reshape(4, HALF)
    moment_one_new = 0.9 * moment_one + 0.1 * reduced_grad
    moment_two_new = 0.95 * moment_two + 0.05 * reduced_grad * reduced_grad
    update = (moment_one_new / (1.0 - 0.9**STEP)) / (
        jnp.sqrt(moment_two_new / (1.0 - 0.95**STEP)) + 1e-08
    )
    master_new = master - 0.001 * (update + 0.1 * master)
    blocks = master_new.reshape(4, NB, BLOCK)
    wscale = jnp.max(jnp.abs(blocks), axis=2) + 1e-06
    wmant = (blocks / wscale[:, :, None]).astype(BF16)
    weights = (wmant.astype(F32) * wscale[:, :, None]).reshape(4, HALF).astype(BF16)

    out = jnp.stack([master_new, moment_one_new, moment_two_new, reduced_grad])
    out_own = jnp.where(first, out[:, :2], out[:, 2:])
    out_other = lax.ppermute(jnp.where(first, out[:, 2:], out[:, :2]), "dp", SWAP)
    out = jnp.where(
        first,
        jnp.concatenate([out_own, out_other], axis=2),
        jnp.concatenate([out_other, out_own], axis=2),
    )

    weights = spread(weights, FAR_GROUPS).reshape(32, HALF)
    weights = spread(weights, NEAR_GROUPS)
    weights_other = lax.ppermute(weights, "dp", SWAP)
    full = place_rows(mine, weights)
    full = place_rows(theirs, weights_other, full)
    return (out[0], out[1], out[2], out[3], full)


def solution(mesh):
    in_specs = (P("dp", None, None), P("dp", None), P("dp", None), P("dp", None))
    out_specs = (P("dp", None), P("dp", None), P("dp", None), P("dp", None), P())
    return jax.shard_map(
        per_device, mesh=mesh, in_specs=in_specs, out_specs=out_specs, check_vma=False
    )
```

```python
import jax
import jax.numpy as jnp
from jax import lax
from jax.experimental import pallas as pl
from jax.experimental.pallas import tpu as pltpu
from jax.sharding import PartitionSpec as P

BLOCK = 128
MBITS = 7
STEP = 20
ROWS = 256
W = 16384
N_DP = 128
HALF = W // 2
NB = HALF // BLOCK
F32 = jnp.float32
BF16 = jnp.bfloat16
F16 = jnp.float16

NEAR = {0: ((0, 1), (3, 2)), 1: ((1, 2), (0, 3))}
FAR = {0: ((0, 3), (1, 2)), 1: ((0, 1), (2, 3))}
PLACE = {0: (0, 2, 3, 1), 1: (0, 1, 2, 3)}
ORDER = {0: (0, 3, 1, 2), 1: (0, 1, 2, 3)}


def device(x, z, y, core):
    return ((x * 4 + z) * 4 + y) * 2 + core


def groups(pairs):
    return [
        [device(x, z, y, core) for x in px for z in pz for y in py]
        for core in (0, 1)
        for px in pairs[core]
        for pz in pairs[core]
        for py in pairs[core]
    ]


NEAR_GROUPS = groups(NEAR)
FAR_GROUPS = groups(FAR)
Y_CORES = [[device(x, z, y, core) for core in (0, 1) for y in range(4)] for x in range(4) for z in range(4)]
X_Z = [[device(x, z, y, core) for x in range(4) for z in range(4)] for y in range(4) for core in (0, 1)]
SWAP = [(d, d ^ 1) for d in range(N_DP)]


def exchange(x, among):
    return lax.all_to_all(x, "dp", 0, 0, axis_index_groups=among)


def spread(x, among):
    return exchange(jnp.broadcast_to(x[None], (len(among[0]), *x.shape)), among)


def max_kernel(core_ref, x_ref, amax_ref, send_ref, buf, left, right, in_sem, out_sem):
    core = core_ref[0]
    rows = ROWS // in_sem.shape[0]
    theirs = pl.ds(pl.multiple_of((1 - core) * HALF, HALF), HALF)
    chunks = [pl.ds(i * rows, rows) for i in range(ROWS // rows)]
    loads = [
        pltpu.make_async_copy(x_ref.at[0, at], buf.at[at], in_sem.at[i])
        for i, at in enumerate(chunks)
    ]
    stores = [
        pltpu.make_async_copy(buf.at[at, theirs], send_ref.at[at], out_sem.at[i])
        for i, at in enumerate(chunks)
    ]
    for load in loads:
        load.start()
    lane = lax.broadcasted_iota(jnp.int32, (rows, 128), 1)
    low = lane < NB
    for i, at in enumerate(chunks):
        loads[i].wait()
        stores[i].start()
        acc = jnp.zeros((rows, 128), F32)
        for b in range(W // BLOCK):
            v = jnp.abs(buf[at, b * BLOCK : (b + 1) * BLOCK].astype(F32))
            acc = jnp.where(lane == b, jnp.max(v, axis=1, keepdims=True), acc)
        rolled = pltpu.roll(acc, NB, 1)
        to = pl.ds(i * rows % 128, rows)
        if i * rows < 128:
            left[to, :], right[to, :] = acc, rolled
        else:
            left[to, :] = jnp.where(low, left[to, :], rolled)
            right[to, :] = jnp.where(low, right[to, :], acc)
    amax_ref[0] = left[...].astype(BF16)
    amax_ref[1] = right[...].astype(BF16)
    for store in stores:
        store.wait()


SMEM = pl.BlockSpec(memory_space=pltpu.SMEM)
VMEM = pl.BlockSpec(memory_space=pltpu.VMEM)
HBM = pl.BlockSpec(memory_space=pltpu.HBM)
PARAMS = pltpu.CompilerParams(vmem_limit_bytes=60 << 20)


def block_max(core, partials, chunks=4):
    return pl.pallas_call(
        max_kernel,
        out_shape=(
            jax.ShapeDtypeStruct((2, 128, 128), BF16),
            jax.ShapeDtypeStruct((ROWS, HALF), BF16),
        ),
        in_specs=[SMEM, HBM],
        out_specs=[VMEM, HBM],
        scratch_shapes=[
            pltpu.VMEM((ROWS, W), BF16),
            pltpu.VMEM((128, 128), F32),
            pltpu.VMEM((128, 128), F32),
            pltpu.SemaphoreType.DMA((chunks,)),
            pltpu.SemaphoreType.DMA((chunks,)),
        ],
        compiler_params=PARAMS,
        name="block_max",
    )(core, partials)


def scale_of(amax):
    scale = jnp.full(amax.shape, 2.0**-20, F32)
    for k in range(-20, 13):
        scale = jnp.where(amax >= 2.0**k, F32(2.0 ** (k + 1)), scale)
    return scale


def mult_of(amax):
    mult = jnp.full(amax.shape, 2.0 ** (MBITS + 20), F32)
    for k in range(-20, 13):
        mult = jnp.where(amax >= 2.0**k, F32(2.0 ** (MBITS - k - 1)), mult)
    return mult


def block_of(at_ref, x, z, y):
    px, pz = at_ref[1 + x], at_ref[1 + z]
    return (px >> 1, pz >> 1, y, px & 1, pz & 1)


def tile_mask(at_ref):
    row = lax.broadcasted_iota(jnp.int32, (8, BLOCK), 0)
    return row < 4 + 4 * at_ref[0], 4 * (1 - at_ref[0])


def quant_kernel(at_ref, x_ref, other_ref, amax_ref, out_ref, own, other, mant, own_sem, other_sem, out_sem):
    chunks = own_sem.shape[0]
    rows = ROWS // chunks
    mine = pl.ds(pl.multiple_of(at_ref[0] * HALF, HALF), HALF)
    loads, stores = [], []
    for i in range(chunks):
        at = pl.ds(i * rows, rows)
        loads.append(
            (
                pltpu.make_async_copy(x_ref.at[0, at, mine], own.at[at], own_sem.at[i]),
                pltpu.make_async_copy(other_ref.at[at], other.at[at], other_sem.at[i]),
            )
        )
        for load in loads[i]:
            load.start()
    keep, turn = tile_mask(at_ref)
    for i in range(chunks):
        at = pl.ds(i * rows, rows)
        low = i * rows % 128
        mult = mult_of(amax_ref[low : low + rows, :].astype(F32))
        for load in loads[i]:
            load.wait()
        for b in range(NB):
            cols = slice(b * BLOCK, (b + 1) * BLOCK)
            lane = b + (NB if i * rows >= 128 else 0)
            m = jnp.broadcast_to(mult[:, lane : lane + 1], (rows, BLOCK))
            v = jnp.floor(own[at, cols].astype(F32) * m + 0.5)
            v = v + jnp.floor(other[at, cols].astype(F32) * m + 0.5)
            for t in range(0, rows // 8, 2):
                p, q = v[t * 8 : t * 8 + 8], v[t * 8 + 8 : t * 8 + 16]
                tile = i * rows // 8 + t
                mant[tile, :, cols] = jnp.where(keep, p, q).astype(BF16)
                mant[tile + 1, :, cols] = pltpu.roll(jnp.where(keep, q, p), turn, 0).astype(BF16)
        for t in range(i * rows // 8, (i + 1) * rows // 8):
            target = out_ref.at[block_of(at_ref, t // 8, t // 2 % 4, t % 2)]
            stores.append(pltpu.make_async_copy(mant.at[t], target, out_sem.at[t]))
            stores[t].start()
    for store in stores:
        store.wait()


def quantise(at, partials, other, amax, chunks=8):
    out = pl.pallas_call(
        quant_kernel,
        out_shape=jax.ShapeDtypeStruct((2, 2, 2, 2, 2, 8, HALF), BF16),
        in_specs=[SMEM, HBM, HBM, VMEM],
        out_specs=HBM,
        scratch_shapes=[
            pltpu.VMEM((ROWS, HALF), BF16),
            pltpu.VMEM((ROWS, HALF), BF16),
            pltpu.VMEM((ROWS // 8, 8, HALF), BF16),
            pltpu.SemaphoreType.DMA((chunks,)),
            pltpu.SemaphoreType.DMA((chunks,)),
            pltpu.SemaphoreType.DMA((ROWS // 8,)),
        ],
        compiler_params=PARAMS,
        name="quantise",
    )(at, partials, other, amax)
    return out.reshape(8, 32, HALF)


def rows_kernel(at_ref, w_ref, *refs):
    out_ref, got, full, in_sem, out_sem = refs[-5:]
    half = pl.ds(pl.multiple_of(at_ref[0] * HALF, HALF), HALF)
    keep, turn = tile_mask(at_ref)
    chunks = [(i >> 2, i >> 1 & 1, i & 1) for i in range(8)]
    loads, stores = [], []
    for i, (jx, jz, ox) in enumerate(chunks):
        source, target = w_ref.at[jx, jz, :, ox], got.at[i]
        loads.append(pltpu.make_async_copy(source, target, in_sem.at[i]))
        loads[i].start()
    for i, (jx, jz, ox) in enumerate(chunks):
        loads[i].wait()
        for oz in (0, 1):
            n = 2 * i + oz
            for b in range(NB):
                cols = slice(b * BLOCK, (b + 1) * BLOCK)
                p = got[i, 0, oz, :, cols].astype(F32)
                q = pltpu.roll(got[i, 1, oz, :, cols].astype(F32), turn, 0)
                full[n, :8, cols] = jnp.where(keep, p, q).astype(BF16)
                full[n, 8:, cols] = jnp.where(keep, q, p).astype(BF16)
            x, z = at_ref[5 + 2 * jx + ox], at_ref[5 + 2 * jz + oz]
            at = pl.ds(pl.multiple_of(x * 64 + z * 16, 16), 16)
            stores.append(pltpu.make_async_copy(full.at[n], out_ref.at[at, half], out_sem.at[n]))
            stores[n].start()
    for store in stores:
        store.wait()


def place_rows(at, w, before=None):
    more = () if before is None else (before,)
    return pl.pallas_call(
        rows_kernel,
        out_shape=jax.ShapeDtypeStruct((ROWS, W), BF16),
        in_specs=[SMEM, HBM, *(HBM for _ in more)],
        out_specs=HBM,
        scratch_shapes=[
            pltpu.VMEM((8, 2, 2, 8, HALF), BF16),
            pltpu.VMEM((16, 16, HALF), BF16),
            pltpu.SemaphoreType.DMA((8,)),
            pltpu.SemaphoreType.DMA((16,)),
        ],
        input_output_aliases={2: 0} if more else {},
        compiler_params=PARAMS,
        name="place_rows",
    )(at, w.reshape(2, 2, 2, 2, 2, 8, HALF), *more)


def per_device(partials, master, moment_one, moment_two):
    d = lax.axis_index("dp")
    core, chip = d & 1, d >> 1
    first = core == 0
    row = chip * 4
    tables = [[c, *(jnp.where(c == 0, t[0][i], t[1][i]) for t in (PLACE, ORDER) for i in range(4))] for c in (core, 1 - core)]
    mine, theirs = (jnp.stack(table) for table in tables)

    amax, send = block_max(core.reshape(1), partials)
    other = lax.ppermute(send, "dp", SWAP)
    amax = jnp.broadcast_to(amax[:, None], (2, 4, 128, 128)).reshape(8, 128, 128)
    amax = jnp.max(exchange(amax, Y_CORES), axis=0)
    amax = jnp.max(spread(amax, X_Z), axis=0)

    state = jnp.stack([master, moment_one, moment_two])
    state_own = lax.dynamic_slice_in_dim(state, core * HALF, HALF, 2)
    state_other = lax.dynamic_slice_in_dim(state, (1 - core) * HALF, HALF, 2)
    state_other = lax.ppermute(state_other, "dp", SWAP)
    state = jnp.where(
        first,
        jnp.concatenate([state_own, state_other], axis=1),
        jnp.concatenate([state_other, state_own], axis=1),
    )
    master, moment_one, moment_two = state

    mant = exchange(quantise(mine, partials, other, amax), NEAR_GROUPS)
    mant = jnp.sum(mant.astype(F32), axis=0).astype(F16).reshape(8, 4, HALF)
    total = jnp.sum(exchange(mant, FAR_GROUPS).astype(F32), axis=0)

    own_amax = lax.dynamic_slice(amax, (row & 127, (row >> 7) * NB), (4, NB))
    scale = scale_of(own_amax.astype(F32))
    factor = scale / (2.0**MBITS * N_DP)
    reduced_grad = (total.reshape(4, NB, BLOCK) * factor[:, :, None]).reshape(4, HALF)
    moment_one_new = 0.9 * moment_one + 0.1 * reduced_grad
    moment_two_new = 0.95 * moment_two + 0.05 * reduced_grad * reduced_grad
    update = (moment_one_new / (1.0 - 0.9**STEP)) / (
        jnp.sqrt(moment_two_new / (1.0 - 0.95**STEP)) + 1e-08
    )
    master_new = master - 0.001 * (update + 0.1 * master)
    blocks = master_new.reshape(4, NB, BLOCK)
    wscale = jnp.max(jnp.abs(blocks), axis=2) + 1e-06
    wmant = (blocks / wscale[:, :, None]).astype(BF16)
    weights = (wmant.astype(F32) * wscale[:, :, None]).reshape(4, HALF).astype(BF16)

    out = jnp.stack([master_new, moment_one_new, moment_two_new, reduced_grad])
    out_own = jnp.where(first, out[:, :2], out[:, 2:])
    out_other = lax.ppermute(jnp.where(first, out[:, 2:], out[:, :2]), "dp", SWAP)
    out = jnp.where(
        first,
        jnp.concatenate([out_own, out_other], axis=2),
        jnp.concatenate([out_other, out_own], axis=2),
    )

    weights = spread(weights, FAR_GROUPS).reshape(32, HALF)
    weights = spread(weights, NEAR_GROUPS)
    weights_other = lax.ppermute(weights, "dp", SWAP)
    full = place_rows(mine, weights)
    full = place_rows(theirs, weights_other, full)
    return (out[0], out[1], out[2], out[3], full)


def solution(mesh):
    in_specs = (P("dp", None, None), P("dp", None), P("dp", None), P("dp", None))
    out_specs = (P("dp", None), P("dp", None), P("dp", None), P("dp", None), P())
    return jax.shard_map(
        per_device, mesh=mesh, in_specs=in_specs, out_specs=out_specs, check_vma=False
    )
```

```python
import jax
import jax.numpy as jnp
from jax import lax
from jax.experimental import pallas as pl
from jax.experimental.pallas import tpu as pltpu
from jax.sharding import PartitionSpec as P

BLOCK = 128
MBITS = 7
STEP = 20
ROWS = 256
W = 16384
N_DP = 128
HALF = W // 2
NB = HALF // BLOCK
F32 = jnp.float32
BF16 = jnp.bfloat16
F16 = jnp.float16

NEAR = {0: ((0, 1), (3, 2)), 1: ((1, 2), (0, 3))}
FAR = {0: ((0, 3), (1, 2)), 1: ((0, 1), (2, 3))}
PLACE = {0: (0, 2, 3, 1), 1: (0, 1, 2, 3)}
BACK = {0: ((0, 3), (1, 2)), 1: ((0, 1), (3, 2))}
ARRIVE = {0: (0, 1, 3, 2), 1: (0, 3, 1, 2)}


def device(x, z, y, core):
    return ((x * 4 + z) * 4 + y) * 2 + core


def groups(pairs):
    return [
        [device(x, z, y, core) for x in px for z in pz for y in py]
        for core in (0, 1)
        for px in pairs[core]
        for pz in pairs[core]
        for py in pairs[core]
    ]


NEAR_GROUPS = groups(NEAR)
FAR_GROUPS = groups(FAR)
BACK_GROUPS = groups(BACK)
Y_CORES = [[device(x, z, y, core) for core in (0, 1) for y in range(4)] for x in range(4) for z in range(4)]
X_Z = [[device(x, z, y, core) for x in range(4) for z in range(4)] for y in range(4) for core in (0, 1)]
SWAP = [(d, d ^ 1) for d in range(N_DP)]


def exchange(x, among):
    return lax.all_to_all(x, "dp", 0, 0, axis_index_groups=among)


def spread(x, among):
    return exchange(jnp.broadcast_to(x[None], (len(among[0]), *x.shape)), among)


def max_kernel(core_ref, x_ref, amax_ref, send_ref, buf, left, right, in_sem, out_sem):
    core = core_ref[0]
    rows = ROWS // in_sem.shape[0]
    theirs = pl.ds(pl.multiple_of((1 - core) * HALF, HALF), HALF)
    chunks = [pl.ds(i * rows, rows) for i in range(ROWS // rows)]
    loads = [
        pltpu.make_async_copy(x_ref.at[0, at], buf.at[at], in_sem.at[i])
        for i, at in enumerate(chunks)
    ]
    stores = [
        pltpu.make_async_copy(buf.at[at, theirs], send_ref.at[at], out_sem.at[i])
        for i, at in enumerate(chunks)
    ]
    for load in loads:
        load.start()
    lane = lax.broadcasted_iota(jnp.int32, (rows, 128), 1)
    low = lane < NB
    for i, at in enumerate(chunks):
        loads[i].wait()
        stores[i].start()
        acc = jnp.zeros((rows, 128), F32)
        for b in range(W // BLOCK):
            v = jnp.abs(buf[at, b * BLOCK : (b + 1) * BLOCK].astype(F32))
            acc = jnp.where(lane == b, jnp.max(v, axis=1, keepdims=True), acc)
        rolled = pltpu.roll(acc, NB, 1)
        to = pl.ds(i * rows % 128, rows)
        if i * rows < 128:
            left[to, :], right[to, :] = acc, rolled
        else:
            left[to, :] = jnp.where(low, left[to, :], rolled)
            right[to, :] = jnp.where(low, right[to, :], acc)
    for j in range(4):
        amax_ref[j] = left[...].astype(BF16)
        amax_ref[4 + j] = right[...].astype(BF16)
    for store in stores:
        store.wait()


SMEM = pl.BlockSpec(memory_space=pltpu.SMEM)
VMEM = pl.BlockSpec(memory_space=pltpu.VMEM)
HBM = pl.BlockSpec(memory_space=pltpu.HBM)
PARAMS = pltpu.CompilerParams(vmem_limit_bytes=60 << 20)


def block_max(core, partials, chunks=4):
    return pl.pallas_call(
        max_kernel,
        out_shape=(
            jax.ShapeDtypeStruct((8, 128, 128), BF16),
            jax.ShapeDtypeStruct((ROWS, HALF), BF16),
        ),
        in_specs=[SMEM, HBM],
        out_specs=[VMEM, HBM],
        scratch_shapes=[
            pltpu.VMEM((ROWS, W), BF16),
            pltpu.VMEM((128, 128), F32),
            pltpu.VMEM((128, 128), F32),
            pltpu.SemaphoreType.DMA((chunks,)),
            pltpu.SemaphoreType.DMA((chunks,)),
        ],
        compiler_params=PARAMS,
        name="block_max",
    )(core, partials)


def scale_of(amax):
    scale = jnp.full(amax.shape, 2.0**-20, F32)
    for k in range(-20, 13):
        scale = jnp.where(amax >= 2.0**k, F32(2.0 ** (k + 1)), scale)
    return scale


def mult_of(amax):
    mult = jnp.full(amax.shape, 2.0 ** (MBITS + 20), F32)
    for k in range(-20, 13):
        mult = jnp.where(amax >= 2.0**k, F32(2.0 ** (MBITS - k - 1)), mult)
    return mult


def pick(core, table, i):
    return jnp.where(core == 0, table[0][i], table[1][i])


def block_of(core, x, z, y):
    px, pz = pick(core, PLACE, x), pick(core, PLACE, z)
    return (px >> 1, pz >> 1, y, px & 1, pz & 1)


def rows_below(limit):
    return lax.broadcasted_iota(jnp.int32, (8, BLOCK), 0) < limit


def quant_kernel(core_ref, x_ref, other_ref, amax_ref, out_ref, own, other, mant, own_sem, other_sem, out_sem):
    chunks = own_sem.shape[0]
    rows = ROWS // chunks
    mine = pl.ds(pl.multiple_of(core_ref[0] * HALF, HALF), HALF)
    loads, stores = [], []
    for i in range(chunks):
        at = pl.ds(i * rows, rows)
        loads.append(
            (
                pltpu.make_async_copy(x_ref.at[0, at, mine], own.at[at], own_sem.at[i]),
                pltpu.make_async_copy(other_ref.at[at], other.at[at], other_sem.at[i]),
            )
        )
        for load in loads[i]:
            load.start()
    keep, turn = rows_below(4 + 4 * core_ref[0]), 4 * (1 - core_ref[0])
    for i in range(chunks):
        at = pl.ds(i * rows, rows)
        low = i * rows % 128
        mult = mult_of(amax_ref[low : low + rows, :].astype(F32))
        for load in loads[i]:
            load.wait()
        for b in range(NB):
            cols = slice(b * BLOCK, (b + 1) * BLOCK)
            lane = b + (NB if i * rows >= 128 else 0)
            m = jnp.broadcast_to(mult[:, lane : lane + 1], (rows, BLOCK))
            v = jnp.floor(own[at, cols].astype(F32) * m + 0.5)
            v = v + jnp.floor(other[at, cols].astype(F32) * m + 0.5)
            for t in range(0, rows // 8, 2):
                p, q = v[t * 8 : t * 8 + 8], v[t * 8 + 8 : t * 8 + 16]
                tile = i * rows // 8 + t
                mant[tile, :, cols] = jnp.where(keep, p, q).astype(BF16)
                mant[tile + 1, :, cols] = pltpu.roll(jnp.where(keep, q, p), turn, 0).astype(BF16)
        for t in range(i * rows // 8, (i + 1) * rows // 8):
            target = out_ref.at[block_of(core_ref[0], t // 8, t // 2 % 4, t % 2)]
            stores.append(pltpu.make_async_copy(mant.at[t], target, out_sem.at[t]))
            stores[t].start()
    for store in stores:
        store.wait()


def quantise(core, partials, other, amax, chunks=8):
    out = pl.pallas_call(
        quant_kernel,
        out_shape=jax.ShapeDtypeStruct((2, 2, 2, 2, 2, 8, HALF), BF16),
        in_specs=[SMEM, HBM, HBM, VMEM],
        out_specs=HBM,
        scratch_shapes=[
            pltpu.VMEM((ROWS, HALF), BF16),
            pltpu.VMEM((ROWS, HALF), BF16),
            pltpu.VMEM((ROWS // 8, 8, HALF), BF16),
            pltpu.SemaphoreType.DMA((chunks,)),
            pltpu.SemaphoreType.DMA((chunks,)),
            pltpu.SemaphoreType.DMA((ROWS // 8,)),
        ],
        compiler_params=PARAMS,
        name="quantise",
    )(core, partials, other, amax)
    return out.reshape(8, 32, HALF)


def rows_kernel(core_ref, w_ref, *refs):
    out_ref, got, full, in_sem, out_sem = refs[-5:]
    half = pl.ds(pl.multiple_of(core_ref[0] * HALF, HALF), HALF)
    keep = rows_below(8 - 4 * core_ref[0])
    chunks = [(i >> 2, i >> 1 & 1, i & 1) for i in range(8)]
    loads, stores = [], []
    for i, (ox, oz, jx) in enumerate(chunks):
        source, target = w_ref.at[ox, oz, :, jx], got.at[i]
        loads.append(pltpu.make_async_copy(source, target, in_sem.at[i]))
        loads[i].start()
    for i, (ox, oz, jx) in enumerate(chunks):
        loads[i].wait()
        for jz in (0, 1):
            n = 2 * i + jz
            for b in range(NB):
                cols = slice(b * BLOCK, (b + 1) * BLOCK)
                p = got[i, 0, jz, :, cols].astype(F32)
                q = pltpu.roll(got[i, 1, jz, :, cols].astype(F32), 4, 0)
                full[n, :8, cols] = jnp.where(keep, p, q).astype(BF16)
                full[n, 8:, cols] = jnp.where(keep, q, p).astype(BF16)
            x = pick(core_ref[0], ARRIVE, 2 * ox + jx)
            z = pick(core_ref[0], ARRIVE, 2 * oz + jz)
            at = pl.ds(pl.multiple_of(x * 64 + z * 16, 16), 16)
            stores.append(pltpu.make_async_copy(full.at[n], out_ref.at[at, half], out_sem.at[n]))
            stores[n].start()
    for store in stores:
        store.wait()


def place_rows(core, w, before=None):
    more = () if before is None else (before,)
    return pl.pallas_call(
        rows_kernel,
        out_shape=jax.ShapeDtypeStruct((ROWS, W), BF16),
        in_specs=[SMEM, HBM, *(HBM for _ in more)],
        out_specs=HBM,
        scratch_shapes=[
            pltpu.VMEM((8, 2, 2, 8, HALF), BF16),
            pltpu.VMEM((16, 16, HALF), BF16),
            pltpu.SemaphoreType.DMA((8,)),
            pltpu.SemaphoreType.DMA((16,)),
        ],
        input_output_aliases={2: 0} if more else {},
        compiler_params=PARAMS,
        name="place_rows",
    )(core, w.reshape(2, 2, 2, 2, 2, 8, HALF), *more)


def per_device(partials, master, moment_one, moment_two):
    d = lax.axis_index("dp")
    core, chip = d & 1, d >> 1
    first = core == 0
    row = chip * 4
    mine, theirs = core.reshape(1), (1 - core).reshape(1)

    amax, send = block_max(mine, partials)
    other = lax.ppermute(send, "dp", SWAP)
    amax = jnp.max(exchange(amax, Y_CORES), axis=0)
    amax = jnp.max(spread(amax, X_Z), axis=0)

    state = jnp.stack([master, moment_one, moment_two])
    state_own = lax.dynamic_slice_in_dim(state, core * HALF, HALF, 2)
    state_other = lax.dynamic_slice_in_dim(state, (1 - core) * HALF, HALF, 2)
    state_other = lax.ppermute(state_other, "dp", SWAP)
    state = jnp.where(
        first,
        jnp.concatenate([state_own, state_other], axis=1),
        jnp.concatenate([state_other, state_own], axis=1),
    )
    master, moment_one, moment_two = state

    mant = exchange(quantise(mine, partials, other, amax), NEAR_GROUPS)
    mant = jnp.sum(mant.astype(F32), axis=0).astype(F16).reshape(8, 4, HALF)
    total = jnp.sum(exchange(mant, FAR_GROUPS).astype(F32), axis=0)

    own_amax = lax.dynamic_slice(amax, (row & 127, (row >> 7) * NB), (4, NB))
    scale = scale_of(own_amax.astype(F32))
    factor = scale / (2.0**MBITS * N_DP)
    reduced_grad = (total.reshape(4, NB, BLOCK) * factor[:, :, None]).reshape(4, HALF)
    moment_one_new = 0.9 * moment_one + 0.1 * reduced_grad
    moment_two_new = 0.95 * moment_two + 0.05 * reduced_grad * reduced_grad
    update = (moment_one_new / (1.0 - 0.9**STEP)) / (
        jnp.sqrt(moment_two_new / (1.0 - 0.95**STEP)) + 1e-08
    )
    master_new = master - 0.001 * (update + 0.1 * master)
    blocks = master_new.reshape(4, NB, BLOCK)
    wscale = jnp.max(jnp.abs(blocks), axis=2) + 1e-06
    wmant = (blocks / wscale[:, :, None]).astype(BF16)
    weights = (wmant.astype(F32) * wscale[:, :, None]).reshape(4, HALF).astype(BF16)

    out = jnp.stack([master_new, moment_one_new, moment_two_new, reduced_grad])
    out_own = jnp.where(first, out[:, :2], out[:, 2:])
    out_other = lax.ppermute(jnp.where(first, out[:, 2:], out[:, :2]), "dp", SWAP)
    out = jnp.where(
        first,
        jnp.concatenate([out_own, out_other], axis=2),
        jnp.concatenate([out_other, out_own], axis=2),
    )

    weights = spread(weights, NEAR_GROUPS).reshape(32, HALF)
    weights = spread(weights, BACK_GROUPS)
    weights_other = lax.ppermute(weights, "dp", SWAP)
    full = place_rows(mine, weights)
    full = place_rows(theirs, weights_other, full)
    return (out[0], out[1], out[2], out[3], full)


def solution(mesh):
    in_specs = (P("dp", None, None), P("dp", None), P("dp", None), P("dp", None))
    out_specs = (P("dp", None), P("dp", None), P("dp", None), P("dp", None), P())
    return jax.shard_map(
        per_device, mesh=mesh, in_specs=in_specs, out_specs=out_specs, check_vma=False
    )
```

```python
import jax
import jax.numpy as jnp
from jax import lax
from jax.experimental import pallas as pl
from jax.experimental.pallas import tpu as pltpu
from jax.sharding import PartitionSpec as P

BLOCK = 128
MBITS = 7
STEP = 20
ROWS = 256
W = 16384
N_DP = 128
HALF = W // 2
NB = HALF // BLOCK
F32 = jnp.float32
BF16 = jnp.bfloat16
F16 = jnp.float16

NEAR = {0: ((0, 1), (3, 2)), 1: ((1, 2), (0, 3))}
FAR = {0: ((0, 3), (1, 2)), 1: ((0, 1), (2, 3))}
PLACE = {0: (0, 2, 3, 1), 1: (0, 1, 2, 3)}
BACK = {0: ((0, 3), (1, 2)), 1: ((0, 1), (3, 2))}
ARRIVE = {0: (0, 1, 3, 2), 1: (0, 3, 1, 2)}


def device(x, z, y, core):
    return ((x * 4 + z) * 4 + y) * 2 + core


def groups(pairs):
    return [
        [device(x, z, y, core) for x in px for z in pz for y in py]
        for core in (0, 1)
        for px in pairs[1 - core]
        for pz in pairs[core]
        for py in pairs[core]
    ]


NEAR_GROUPS = groups(NEAR)
FAR_GROUPS = groups(FAR)
BACK_GROUPS = groups(BACK)
Y_CORES = [[device(x, z, y, core) for core in (0, 1) for y in range(4)] for x in range(4) for z in range(4)]
X_Z = [[device(x, z, y, core) for x in range(4) for z in range(4)] for y in range(4) for core in (0, 1)]
SWAP = [(d, d ^ 1) for d in range(N_DP)]


def exchange(x, among):
    return lax.all_to_all(x, "dp", 0, 0, axis_index_groups=among)


def spread(x, among):
    return exchange(jnp.broadcast_to(x[None], (len(among[0]), *x.shape)), among)


def max_kernel(core_ref, x_ref, amax_ref, send_ref, buf, left, right, in_sem, out_sem):
    core = core_ref[0]
    theirs = pl.ds(pl.multiple_of((1 - core) * HALF, HALF), HALF)
    starts = (0, 32, 64, 128, 192, ROWS)
    chunks = [pl.ds(i, j - i) for i, j in zip(starts, starts[1:])]
    loads = [
        pltpu.make_async_copy(x_ref.at[0, at], buf.at[at], in_sem.at[i])
        for i, at in enumerate(chunks)
    ]
    stores = [
        pltpu.make_async_copy(buf.at[at, theirs], send_ref.at[at], out_sem.at[i])
        for i, at in enumerate(chunks)
    ]
    for load in loads:
        load.start()
    for i, at in enumerate(chunks):
        lane = lax.broadcasted_iota(jnp.int32, (at.size, 128), 1)
        loads[i].wait()
        stores[i].start()
        acc = jnp.zeros((at.size, 128), F32)
        for b in range(W // BLOCK):
            v = jnp.abs(buf[at, b * BLOCK : (b + 1) * BLOCK].astype(F32))
            acc = jnp.where(lane == b, jnp.max(v, axis=1, keepdims=True), acc)
        rolled, low = pltpu.roll(acc, NB, 1), lane < NB
        to = pl.ds(at.start % 128, at.size)
        if at.start < 128:
            left[to, :], right[to, :] = acc, rolled
        else:
            left[to, :] = jnp.where(low, left[to, :], rolled)
            right[to, :] = jnp.where(low, right[to, :], acc)
    for j in range(4):
        amax_ref[j] = left[...].astype(BF16)
        amax_ref[4 + j] = right[...].astype(BF16)
    for store in stores:
        store.wait()


SMEM = pl.BlockSpec(memory_space=pltpu.SMEM)
VMEM = pl.BlockSpec(memory_space=pltpu.VMEM)
HBM = pl.BlockSpec(memory_space=pltpu.HBM)
PARAMS = pltpu.CompilerParams(vmem_limit_bytes=60 << 20)


def block_max(core, partials, chunks=5):
    return pl.pallas_call(
        max_kernel,
        out_shape=(
            jax.ShapeDtypeStruct((8, 128, 128), BF16),
            jax.ShapeDtypeStruct((ROWS, HALF), BF16),
        ),
        in_specs=[SMEM, HBM],
        out_specs=[VMEM, HBM],
        scratch_shapes=[
            pltpu.VMEM((ROWS, W), BF16),
            pltpu.VMEM((128, 128), F32),
            pltpu.VMEM((128, 128), F32),
            pltpu.SemaphoreType.DMA((chunks,)),
            pltpu.SemaphoreType.DMA((chunks,)),
        ],
        compiler_params=PARAMS,
        name="block_max",
    )(core, partials)


def scale_of(amax):
    scale = jnp.full(amax.shape, 2.0**-20, F32)
    for k in range(-20, 13):
        scale = jnp.where(amax >= 2.0**k, F32(2.0 ** (k + 1)), scale)
    return scale


def mult_of(amax):
    mult = jnp.full(amax.shape, 2.0 ** (MBITS + 20), F32)
    for k in range(-20, 13):
        mult = jnp.where(amax >= 2.0**k, F32(2.0 ** (MBITS - k - 1)), mult)
    return mult


def pick(core, table, i):
    return jnp.where(core == 0, table[0][i], table[1][i])


def block_of(core, x, z, y):
    px, pz = pick(1 - core, PLACE, x), pick(core, PLACE, z)
    return (px >> 1, pz >> 1, y, px & 1, pz & 1)


def rows_below(limit):
    return lax.broadcasted_iota(jnp.int32, (8, BLOCK), 0) < limit


def quant_kernel(core_ref, x_ref, other_ref, amax_ref, out_ref, own, other, mant, own_sem, other_sem, out_sem):
    chunks = own_sem.shape[0]
    rows = ROWS // chunks
    mine = pl.ds(pl.multiple_of(core_ref[0] * HALF, HALF), HALF)
    loads, stores = [], []
    for i in range(chunks):
        at = pl.ds(i * rows, rows)
        loads.append(
            (
                pltpu.make_async_copy(x_ref.at[0, at, mine], own.at[at], own_sem.at[i]),
                pltpu.make_async_copy(other_ref.at[at], other.at[at], other_sem.at[i]),
            )
        )
        for load in loads[i]:
            load.start()
    keep, turn = rows_below(4 + 4 * core_ref[0]), 4 * (1 - core_ref[0])
    for i in range(chunks):
        at = pl.ds(i * rows, rows)
        low = i * rows % 128
        mult = mult_of(amax_ref[low : low + rows, :].astype(F32))
        for load in loads[i]:
            load.wait()
        for b in range(NB):
            cols = slice(b * BLOCK, (b + 1) * BLOCK)
            lane = b + (NB if i * rows >= 128 else 0)
            m = jnp.broadcast_to(mult[:, lane : lane + 1], (rows, BLOCK))
            v = jnp.floor(own[at, cols].astype(F32) * m + 0.5)
            v = v + jnp.floor(other[at, cols].astype(F32) * m + 0.5)
            for t in range(0, rows // 8, 2):
                p, q = v[t * 8 : t * 8 + 8], v[t * 8 + 8 : t * 8 + 16]
                tile = i * rows // 8 + t
                mant[tile, :, cols] = jnp.where(keep, p, q).astype(BF16)
                mant[tile + 1, :, cols] = pltpu.roll(jnp.where(keep, q, p), turn, 0).astype(BF16)
        for t in range(i * rows // 8, (i + 1) * rows // 8):
            target = out_ref.at[block_of(core_ref[0], t // 8, t // 2 % 4, t % 2)]
            stores.append(pltpu.make_async_copy(mant.at[t], target, out_sem.at[t]))
            stores[t].start()
    for store in stores:
        store.wait()


def quantise(core, partials, other, amax, chunks=8):
    out = pl.pallas_call(
        quant_kernel,
        out_shape=jax.ShapeDtypeStruct((2, 2, 2, 2, 2, 8, HALF), BF16),
        in_specs=[SMEM, HBM, HBM, VMEM],
        out_specs=HBM,
        scratch_shapes=[
            pltpu.VMEM((ROWS, HALF), BF16),
            pltpu.VMEM((ROWS, HALF), BF16),
            pltpu.VMEM((ROWS // 8, 8, HALF), BF16),
            pltpu.SemaphoreType.DMA((chunks,)),
            pltpu.SemaphoreType.DMA((chunks,)),
            pltpu.SemaphoreType.DMA((ROWS // 8,)),
        ],
        compiler_params=PARAMS,
        name="quantise",
    )(core, partials, other, amax)
    return out.reshape(8, 32, HALF)


def rows_kernel(core_ref, w_ref, *refs):
    out_ref, got, full, in_sem, out_sem = refs[-5:]
    half = pl.ds(pl.multiple_of(core_ref[0] * HALF, HALF), HALF)
    keep = rows_below(8 - 4 * core_ref[0])
    chunks = [(i >> 2, i >> 1 & 1, i & 1) for i in range(8)]
    loads, stores = [], []
    for i, (ox, oz, jx) in enumerate(chunks):
        source, target = w_ref.at[ox, oz, :, jx], got.at[i]
        loads.append(pltpu.make_async_copy(source, target, in_sem.at[i]))
        loads[i].start()
    for i, (ox, oz, jx) in enumerate(chunks):
        loads[i].wait()
        for jz in (0, 1):
            n = 2 * i + jz
            for b in range(NB):
                cols = slice(b * BLOCK, (b + 1) * BLOCK)
                p = got[i, 0, jz, :, cols].astype(F32)
                q = pltpu.roll(got[i, 1, jz, :, cols].astype(F32), 4, 0)
                full[n, :8, cols] = jnp.where(keep, p, q).astype(BF16)
                full[n, 8:, cols] = jnp.where(keep, q, p).astype(BF16)
            x = pick(1 - core_ref[0], ARRIVE, 2 * ox + jx)
            z = pick(core_ref[0], ARRIVE, 2 * oz + jz)
            at = pl.ds(pl.multiple_of(x * 64 + z * 16, 16), 16)
            stores.append(pltpu.make_async_copy(full.at[n], out_ref.at[at, half], out_sem.at[n]))
            stores[n].start()
    for store in stores:
        store.wait()


def place_rows(core, w, before=None):
    more = () if before is None else (before,)
    return pl.pallas_call(
        rows_kernel,
        out_shape=jax.ShapeDtypeStruct((ROWS, W), BF16),
        in_specs=[SMEM, HBM, *(HBM for _ in more)],
        out_specs=HBM,
        scratch_shapes=[
            pltpu.VMEM((8, 2, 2, 8, HALF), BF16),
            pltpu.VMEM((16, 16, HALF), BF16),
            pltpu.SemaphoreType.DMA((8,)),
            pltpu.SemaphoreType.DMA((16,)),
        ],
        input_output_aliases={2: 0} if more else {},
        compiler_params=PARAMS,
        name="place_rows",
    )(core, w.reshape(2, 2, 2, 2, 2, 8, HALF), *more)


def per_device(partials, master, moment_one, moment_two):
    d = lax.axis_index("dp")
    core, chip = d & 1, d >> 1
    first = core == 0
    row = chip * 4
    mine, theirs = core.reshape(1), (1 - core).reshape(1)

    amax, send = block_max(mine, partials)
    other = lax.ppermute(send, "dp", SWAP)
    amax = jnp.max(exchange(amax, Y_CORES), axis=0)
    amax = jnp.max(spread(amax, X_Z), axis=0)

    state = jnp.stack([master, moment_one, moment_two])
    state_own = lax.dynamic_slice_in_dim(state, core * HALF, HALF, 2)
    state_other = lax.dynamic_slice_in_dim(state, (1 - core) * HALF, HALF, 2)
    state_other = lax.ppermute(state_other, "dp", SWAP)
    state = jnp.where(
        first,
        jnp.concatenate([state_own, state_other], axis=1),
        jnp.concatenate([state_other, state_own], axis=1),
    )
    master, moment_one, moment_two = state

    mant = exchange(quantise(mine, partials, other, amax), NEAR_GROUPS)
    mant = jnp.sum(mant.astype(F32), axis=0).astype(F16).reshape(8, 4, HALF)
    total = jnp.sum(exchange(mant, FAR_GROUPS).astype(F32), axis=0)

    own_amax = lax.dynamic_slice(amax, (row & 127, (row >> 7) * NB), (4, NB))
    scale = scale_of(own_amax.astype(F32))
    factor = scale / (2.0**MBITS * N_DP)
    reduced_grad = (total.reshape(4, NB, BLOCK) * factor[:, :, None]).reshape(4, HALF)
    moment_one_new = 0.9 * moment_one + 0.1 * reduced_grad
    moment_two_new = 0.95 * moment_two + 0.05 * reduced_grad * reduced_grad
    update = (moment_one_new / (1.0 - 0.9**STEP)) / (
        jnp.sqrt(moment_two_new / (1.0 - 0.95**STEP)) + 1e-08
    )
    master_new = master - 0.001 * (update + 0.1 * master)
    blocks = master_new.reshape(4, NB, BLOCK)
    wscale = jnp.max(jnp.abs(blocks), axis=2) + 1e-06
    wmant = (blocks / wscale[:, :, None]).astype(BF16)
    weights = (wmant.astype(F32) * wscale[:, :, None]).reshape(4, HALF).astype(BF16)

    out = jnp.stack([master_new, moment_one_new, moment_two_new, reduced_grad])
    out_own = jnp.where(first, out[:, :2], out[:, 2:])
    out_other = lax.ppermute(jnp.where(first, out[:, 2:], out[:, :2]), "dp", SWAP)
    out = jnp.where(
        first,
        jnp.concatenate([out_own, out_other], axis=2),
        jnp.concatenate([out_other, out_own], axis=2),
    )

    weights = spread(weights, NEAR_GROUPS).reshape(32, HALF)
    weights = spread(weights, BACK_GROUPS)
    weights_other = lax.ppermute(weights, "dp", SWAP)
    full = place_rows(mine, weights)
    full = place_rows(theirs, weights_other, full)
    return (out[0], out[1], out[2], out[3], full)


def solution(mesh):
    in_specs = (P("dp", None, None), P("dp", None), P("dp", None), P("dp", None))
    out_specs = (P("dp", None), P("dp", None), P("dp", None), P("dp", None), P())
    return jax.shard_map(
        per_device, mesh=mesh, in_specs=in_specs, out_specs=out_specs, check_vma=False
    )
```

```python
import jax
import jax.numpy as jnp
from jax import lax
from jax.experimental import pallas as pl
from jax.experimental.pallas import tpu as pltpu
from jax.sharding import PartitionSpec as P

BLOCK = 128
MBITS = 7
STEP = 20
ROWS = 256
W = 16384
N_DP = 128
HALF = W // 2
NB = HALF // BLOCK
F32 = jnp.float32
BF16 = jnp.bfloat16
F16 = jnp.float16

NEAR = {0: ((0, 1), (3, 2)), 1: ((1, 2), (0, 3))}
FAR = {0: ((0, 3), (1, 2)), 1: ((0, 1), (2, 3))}
PLACE = {0: (0, 2, 3, 1), 1: (0, 1, 2, 3)}
BACK = {0: ((0, 3), (1, 2)), 1: ((0, 1), (3, 2))}
ARRIVE = {0: (0, 1, 3, 2), 1: (0, 3, 1, 2)}


def device(x, z, y, core):
    return ((x * 4 + z) * 4 + y) * 2 + core


def groups(pairs):
    return [
        [device(x, z, y, core) for x in px for z in pz for y in py]
        for core in (0, 1)
        for px in pairs[1 - core]
        for pz in pairs[core]
        for py in pairs[core]
    ]


NEAR_GROUPS = groups(NEAR)
FAR_GROUPS = groups(FAR)
BACK_GROUPS = groups(BACK)
Y_CORES = [[device(x, z, y, core) for core in (0, 1) for y in range(4)] for x in range(4) for z in range(4)]
X_RING = [[device(x, z, y, core) for x in range(4)] for z in range(4) for y in range(4) for core in (0, 1)]
Z_RING = [[device(x, z, y, core) for z in range(4)] for x in range(4) for y in range(4) for core in (0, 1)]
SWAP = [(d, d ^ 1) for d in range(N_DP)]


def exchange(x, among):
    return lax.all_to_all(x, "dp", 0, 0, axis_index_groups=among)


def spread(x, among):
    return exchange(jnp.broadcast_to(x[None], (len(among[0]), *x.shape)), among)


def max_kernel(core_ref, x_ref, amax_ref, send_ref, buf, left, right, in_sem, out_sem):
    core = core_ref[0]
    theirs = pl.ds(pl.multiple_of((1 - core) * HALF, HALF), HALF)
    starts = (0, 32, 64, 128, 192, ROWS)
    chunks = [pl.ds(i, j - i) for i, j in zip(starts, starts[1:])]
    loads = [
        pltpu.make_async_copy(x_ref.at[0, at], buf.at[at], in_sem.at[i])
        for i, at in enumerate(chunks)
    ]
    stores = [
        pltpu.make_async_copy(buf.at[at, theirs], send_ref.at[at], out_sem.at[i])
        for i, at in enumerate(chunks)
    ]
    for load in loads:
        load.start()
    for i, at in enumerate(chunks):
        lane = lax.broadcasted_iota(jnp.int32, (at.size, 128), 1)
        loads[i].wait()
        stores[i].start()
        acc = jnp.zeros((at.size, 128), F32)
        for b in range(W // BLOCK):
            v = jnp.abs(buf[at, b * BLOCK : (b + 1) * BLOCK].astype(F32))
            acc = jnp.where(lane == b, jnp.max(v, axis=1, keepdims=True), acc)
        rolled, low = pltpu.roll(acc, NB, 1), lane < NB
        to = pl.ds(at.start % 128, at.size)
        if at.start < 128:
            left[to, :], right[to, :] = acc, rolled
        else:
            left[to, :] = jnp.where(low, left[to, :], rolled)
            right[to, :] = jnp.where(low, right[to, :], acc)
    for j in range(4):
        amax_ref[j] = left[...].astype(BF16)
        amax_ref[4 + j] = right[...].astype(BF16)
    for store in stores:
        store.wait()


SMEM = pl.BlockSpec(memory_space=pltpu.SMEM)
VMEM = pl.BlockSpec(memory_space=pltpu.VMEM)
HBM = pl.BlockSpec(memory_space=pltpu.HBM)
PARAMS = pltpu.CompilerParams(vmem_limit_bytes=60 << 20)


def block_max(core, partials, chunks=5):
    return pl.pallas_call(
        max_kernel,
        out_shape=(
            jax.ShapeDtypeStruct((8, 128, 128), BF16),
            jax.ShapeDtypeStruct((ROWS, HALF), BF16),
        ),
        in_specs=[SMEM, HBM],
        out_specs=[VMEM, HBM],
        scratch_shapes=[
            pltpu.VMEM((ROWS, W), BF16),
            pltpu.VMEM((128, 128), F32),
            pltpu.VMEM((128, 128), F32),
            pltpu.SemaphoreType.DMA((chunks,)),
            pltpu.SemaphoreType.DMA((chunks,)),
        ],
        compiler_params=PARAMS,
        name="block_max",
    )(core, partials)


def scale_of(amax):
    scale = jnp.full(amax.shape, 2.0**-20, F32)
    for k in range(-20, 13):
        scale = jnp.where(amax >= 2.0**k, F32(2.0 ** (k + 1)), scale)
    return scale


def mult_of(amax):
    mult = jnp.full(amax.shape, 2.0 ** (MBITS + 20), F32)
    for k in range(-20, 13):
        mult = jnp.where(amax >= 2.0**k, F32(2.0 ** (MBITS - k - 1)), mult)
    return mult


def pick(core, table, i):
    return jnp.where(core == 0, table[0][i], table[1][i])


def block_of(core, x, z, y):
    px, pz = pick(1 - core, PLACE, x), pick(core, PLACE, z)
    return (px >> 1, pz >> 1, y, px & 1, pz & 1)


def rows_below(limit):
    return lax.broadcasted_iota(jnp.int32, (8, BLOCK), 0) < limit


def quant_kernel(core_ref, x_ref, other_ref, amax_ref, out_ref, own, other, mant, own_sem, other_sem, out_sem):
    chunks = own_sem.shape[0]
    rows = ROWS // chunks
    mine = pl.ds(pl.multiple_of(core_ref[0] * HALF, HALF), HALF)
    loads, stores = [], []
    for i in range(chunks):
        at = pl.ds(i * rows, rows)
        loads.append(
            (
                pltpu.make_async_copy(x_ref.at[0, at, mine], own.at[at], own_sem.at[i]),
                pltpu.make_async_copy(other_ref.at[at], other.at[at], other_sem.at[i]),
            )
        )
        for load in loads[i]:
            load.start()
    keep, turn = rows_below(4 + 4 * core_ref[0]), 4 * (1 - core_ref[0])
    for i in range(chunks):
        at = pl.ds(i * rows, rows)
        low = i * rows % 128
        mult = mult_of(amax_ref[low : low + rows, :].astype(F32))
        for load in loads[i]:
            load.wait()
        for b in range(NB):
            cols = slice(b * BLOCK, (b + 1) * BLOCK)
            lane = b + (NB if i * rows >= 128 else 0)
            m = jnp.broadcast_to(mult[:, lane : lane + 1], (rows, BLOCK))
            v = jnp.floor(own[at, cols].astype(F32) * m + 0.5)
            v = v + jnp.floor(other[at, cols].astype(F32) * m + 0.5)
            for t in range(0, rows // 8, 2):
                p, q = v[t * 8 : t * 8 + 8], v[t * 8 + 8 : t * 8 + 16]
                tile = i * rows // 8 + t
                mant[tile, :, cols] = jnp.where(keep, p, q).astype(BF16)
                mant[tile + 1, :, cols] = pltpu.roll(jnp.where(keep, q, p), turn, 0).astype(BF16)
        for t in range(i * rows // 8, (i + 1) * rows // 8):
            target = out_ref.at[block_of(core_ref[0], t // 8, t // 2 % 4, t % 2)]
            stores.append(pltpu.make_async_copy(mant.at[t], target, out_sem.at[t]))
            stores[t].start()
    for store in stores:
        store.wait()


def quantise(core, partials, other, amax, chunks=8):
    out = pl.pallas_call(
        quant_kernel,
        out_shape=jax.ShapeDtypeStruct((2, 2, 2, 2, 2, 8, HALF), BF16),
        in_specs=[SMEM, HBM, HBM, VMEM],
        out_specs=HBM,
        scratch_shapes=[
            pltpu.VMEM((ROWS, HALF), BF16),
            pltpu.VMEM((ROWS, HALF), BF16),
            pltpu.VMEM((ROWS // 8, 8, HALF), BF16),
            pltpu.SemaphoreType.DMA((chunks,)),
            pltpu.SemaphoreType.DMA((chunks,)),
            pltpu.SemaphoreType.DMA((ROWS // 8,)),
        ],
        compiler_params=PARAMS,
        name="quantise",
    )(core, partials, other, amax)
    return out.reshape(8, 32, HALF)


def rows_kernel(core_ref, w_ref, *refs):
    out_ref, full, out_sem = refs[-3:]
    half = pl.ds(pl.multiple_of(core_ref[0] * HALF, HALF), HALF)
    keep = rows_below(8 - 4 * core_ref[0])
    chunks = [(i >> 2, i >> 1 & 1, i & 1) for i in range(8)]
    stores = []
    for i, (ox, oz, jx) in enumerate(chunks):
        for jz in (0, 1):
            n = 2 * i + jz
            for b in range(NB):
                cols = slice(b * BLOCK, (b + 1) * BLOCK)
                p = w_ref[ox, oz, 0, jx, jz, :, cols].astype(F32)
                q = pltpu.roll(w_ref[ox, oz, 1, jx, jz, :, cols].astype(F32), 4, 0)
                full[n, :8, cols] = jnp.where(keep, p, q).astype(BF16)
                full[n, 8:, cols] = jnp.where(keep, q, p).astype(BF16)
            x = pick(1 - core_ref[0], ARRIVE, 2 * ox + jx)
            z = pick(core_ref[0], ARRIVE, 2 * oz + jz)
            at = pl.ds(pl.multiple_of(x * 64 + z * 16, 16), 16)
            stores.append(pltpu.make_async_copy(full.at[n], out_ref.at[at, half], out_sem.at[n]))
            stores[n].start()
    for store in stores:
        store.wait()


def place_rows(core, w, before=None):
    more = () if before is None else (before,)
    return pl.pallas_call(
        rows_kernel,
        out_shape=jax.ShapeDtypeStruct((ROWS, W), BF16),
        in_specs=[SMEM, VMEM, *(HBM for _ in more)],
        out_specs=HBM,
        scratch_shapes=[
            pltpu.VMEM((16, 16, HALF), BF16),
            pltpu.SemaphoreType.DMA((16,)),
        ],
        input_output_aliases={2: 0} if more else {},
        compiler_params=pltpu.CompilerParams(vmem_limit_bytes=24 << 20),
        name="place_rows",
    )(core, w.reshape(2, 2, 2, 2, 2, 8, HALF), *more)


def per_device(partials, master, moment_one, moment_two):
    d = lax.axis_index("dp")
    core, chip = d & 1, d >> 1
    first = core == 0
    row = chip * 4
    mine, theirs = core.reshape(1), (1 - core).reshape(1)

    amax, send = block_max(mine, partials)
    other = lax.ppermute(send, "dp", SWAP)
    amax = jnp.max(exchange(amax, Y_CORES), axis=0)
    amax = jnp.max(spread(amax, X_RING), axis=0)
    amax = jnp.max(spread(amax, Z_RING), axis=0)

    state = jnp.stack([master, moment_one, moment_two])
    state_own = lax.dynamic_slice_in_dim(state, core * HALF, HALF, 2)
    state_other = lax.dynamic_slice_in_dim(state, (1 - core) * HALF, HALF, 2)
    state_other = lax.ppermute(state_other, "dp", SWAP)
    state = jnp.where(
        first,
        jnp.concatenate([state_own, state_other], axis=1),
        jnp.concatenate([state_other, state_own], axis=1),
    )
    master, moment_one, moment_two = state

    mant = exchange(quantise(mine, partials, other, amax), NEAR_GROUPS)
    mant = jnp.sum(mant.astype(F32), axis=0).astype(F16).reshape(8, 4, HALF)
    total = jnp.sum(exchange(mant, FAR_GROUPS).astype(F32), axis=0)

    own_amax = lax.dynamic_slice(amax, (row & 127, (row >> 7) * NB), (4, NB))
    scale = scale_of(own_amax.astype(F32))
    factor = scale / (2.0**MBITS * N_DP)
    reduced_grad = (total.reshape(4, NB, BLOCK) * factor[:, :, None]).reshape(4, HALF)
    moment_one_new = 0.9 * moment_one + 0.1 * reduced_grad
    moment_two_new = 0.95 * moment_two + 0.05 * reduced_grad * reduced_grad
    update = (moment_one_new / (1.0 - 0.9**STEP)) / (
        jnp.sqrt(moment_two_new / (1.0 - 0.95**STEP)) + 1e-08
    )
    master_new = master - 0.001 * (update + 0.1 * master)
    blocks = master_new.reshape(4, NB, BLOCK)
    wscale = jnp.max(jnp.abs(blocks), axis=2) + 1e-06
    wmant = (blocks / wscale[:, :, None]).astype(BF16)
    weights = (wmant.astype(F32) * wscale[:, :, None]).reshape(4, HALF).astype(BF16)

    out = jnp.stack([master_new, moment_one_new, moment_two_new, reduced_grad])
    out_own = jnp.where(first, out[:, :2], out[:, 2:])
    out_other = lax.ppermute(jnp.where(first, out[:, 2:], out[:, :2]), "dp", SWAP)
    out = jnp.where(
        first,
        jnp.concatenate([out_own, out_other], axis=2),
        jnp.concatenate([out_other, out_own], axis=2),
    )

    weights = spread(weights, NEAR_GROUPS).reshape(32, HALF)
    weights = spread(weights, BACK_GROUPS)
    weights_other = lax.ppermute(weights, "dp", SWAP)
    full = place_rows(mine, weights)
    full = place_rows(theirs, weights_other, full)
    return (out[0], out[1], out[2], out[3], full)


def solution(mesh):
    in_specs = (P("dp", None, None), P("dp", None), P("dp", None), P("dp", None))
    out_specs = (P("dp", None), P("dp", None), P("dp", None), P("dp", None), P())
    return jax.shard_map(
        per_device, mesh=mesh, in_specs=in_specs, out_specs=out_specs, check_vma=False
    )
```

```python
import jax
import jax.numpy as jnp
from jax import lax
from jax.experimental import pallas as pl
from jax.experimental.pallas import tpu as pltpu
from jax.sharding import PartitionSpec as P

BLOCK = 128
MBITS = 7
STEP = 20
ROWS = 256
W = 16384
N_DP = 128
HALF = W // 2
NB = HALF // BLOCK
F32 = jnp.float32
BF16 = jnp.bfloat16
F16 = jnp.float16

NEAR = {0: ((0, 1), (3, 2)), 1: ((1, 2), (0, 3))}
FAR = {0: ((0, 3), (1, 2)), 1: ((0, 1), (2, 3))}
PLACE = {0: (0, 2, 3, 1), 1: (0, 1, 2, 3)}
BACK = {0: ((0, 3), (1, 2)), 1: ((0, 1), (3, 2))}
ARRIVE = {0: (0, 1, 3, 2), 1: (0, 3, 1, 2)}


def device(x, z, y, core):
    return ((x * 4 + z) * 4 + y) * 2 + core


def groups(pairs):
    return [
        [device(x, z, y, core) for x in px for z in pz for y in py]
        for core in (0, 1)
        for px in pairs[1 - core]
        for pz in pairs[core]
        for py in pairs[core]
    ]


NEAR_GROUPS = groups(NEAR)
FAR_GROUPS = groups(FAR)
BACK_GROUPS = groups(BACK)
Y_CORES = [[device(x, z, y, core) for core in (0, 1) for y in range(4)] for x in range(4) for z in range(4)]
X_Z = [[device(x, z, y, core) for x in range(4) for z in range(4)] for y in range(4) for core in (0, 1)]
SWAP = [(d, d ^ 1) for d in range(N_DP)]


def exchange(x, among):
    return lax.all_to_all(x, "dp", 0, 0, axis_index_groups=among)


def spread(x, among):
    return exchange(jnp.broadcast_to(x[None], (len(among[0]), *x.shape)), among)


def max_kernel(core_ref, x_ref, amax_ref, send_ref, buf, left, right, in_sem, out_sem):
    core = core_ref[0]
    theirs = pl.ds(pl.multiple_of((1 - core) * HALF, HALF), HALF)
    starts = (0, 32, 64, 128, 192, ROWS)
    chunks = [pl.ds(i, j - i) for i, j in zip(starts, starts[1:])]
    loads = [
        pltpu.make_async_copy(x_ref.at[0, at], buf.at[at], in_sem.at[i])
        for i, at in enumerate(chunks)
    ]
    stores = [
        pltpu.make_async_copy(buf.at[at, theirs], send_ref.at[at], out_sem.at[i])
        for i, at in enumerate(chunks)
    ]
    for load in loads:
        load.start()
    for i, at in enumerate(chunks):
        lane = lax.broadcasted_iota(jnp.int32, (at.size, 128), 1)
        loads[i].wait()
        stores[i].start()
        acc = jnp.zeros((at.size, 128), F32)
        for b in range(W // BLOCK):
            v = jnp.abs(buf[at, b * BLOCK : (b + 1) * BLOCK].astype(F32))
            acc = jnp.where(lane == b, jnp.max(v, axis=1, keepdims=True), acc)
        rolled, low = pltpu.roll(acc, NB, 1), lane < NB
        to = pl.ds(at.start % 128, at.size)
        if at.start < 128:
            left[to, :], right[to, :] = acc, rolled
        else:
            left[to, :] = jnp.where(low, left[to, :], rolled)
            right[to, :] = jnp.where(low, right[to, :], acc)
    for j in range(4):
        amax_ref[j] = left[...].astype(BF16)
        amax_ref[4 + j] = right[...].astype(BF16)
    for store in stores:
        store.wait()


SMEM = pl.BlockSpec(memory_space=pltpu.SMEM)
VMEM = pl.BlockSpec(memory_space=pltpu.VMEM)
HBM = pl.BlockSpec(memory_space=pltpu.HBM)
PARAMS = pltpu.CompilerParams(vmem_limit_bytes=60 << 20)


def block_max(core, partials, chunks=5):
    return pl.pallas_call(
        max_kernel,
        out_shape=(
            jax.ShapeDtypeStruct((8, 128, 128), BF16),
            jax.ShapeDtypeStruct((ROWS, HALF), BF16),
        ),
        in_specs=[SMEM, HBM],
        out_specs=[VMEM, HBM],
        scratch_shapes=[
            pltpu.VMEM((ROWS, W), BF16),
            pltpu.VMEM((128, 128), F32),
            pltpu.VMEM((128, 128), F32),
            pltpu.SemaphoreType.DMA((chunks,)),
            pltpu.SemaphoreType.DMA((chunks,)),
        ],
        compiler_params=PARAMS,
        name="block_max",
    )(core, partials)


def scale_of(amax):
    scale = jnp.full(amax.shape, 2.0**-20, F32)
    for k in range(-20, 13):
        scale = jnp.where(amax >= 2.0**k, F32(2.0 ** (k + 1)), scale)
    return scale


def mult_of(amax):
    mult = jnp.full(amax.shape, 2.0 ** (MBITS + 20), F32)
    for k in range(-20, 13):
        mult = jnp.where(amax >= 2.0**k, F32(2.0 ** (MBITS - k - 1)), mult)
    return mult


def pick(core, table, i):
    return jnp.where(core == 0, table[0][i], table[1][i])


def block_of(core, x, z, y):
    px, pz = pick(1 - core, PLACE, x), pick(core, PLACE, z)
    return (px >> 1, pz >> 1, y, px & 1, pz & 1)


def rows_below(limit):
    return lax.broadcasted_iota(jnp.int32, (8, BLOCK), 0) < limit


def quant_kernel(core_ref, x_ref, other_ref, amax_ref, out_ref, own, other, mant, own_sem, other_sem, out_sem):
    chunks = own_sem.shape[0]
    rows = ROWS // chunks
    mine = pl.ds(pl.multiple_of(core_ref[0] * HALF, HALF), HALF)
    loads, stores = [], []
    for i in range(chunks):
        at = pl.ds(i * rows, rows)
        loads.append(
            (
                pltpu.make_async_copy(x_ref.at[0, at, mine], own.at[at], own_sem.at[i]),
                pltpu.make_async_copy(other_ref.at[at], other.at[at], other_sem.at[i]),
            )
        )
        for load in loads[i]:
            load.start()
    keep, turn = rows_below(4 + 4 * core_ref[0]), 4 * (1 - core_ref[0])
    for i in range(chunks):
        at = pl.ds(i * rows, rows)
        low = i * rows % 128
        mult = mult_of(amax_ref[low : low + rows, :].astype(F32))
        for load in loads[i]:
            load.wait()
        for b in range(NB):
            cols = slice(b * BLOCK, (b + 1) * BLOCK)
            lane = b + (NB if i * rows >= 128 else 0)
            m = jnp.broadcast_to(mult[:, lane : lane + 1], (rows, BLOCK))
            v = jnp.floor(own[at, cols].astype(F32) * m + 0.5)
            v = v + jnp.floor(other[at, cols].astype(F32) * m + 0.5)
            for t in range(0, rows // 8, 2):
                p, q = v[t * 8 : t * 8 + 8], v[t * 8 + 8 : t * 8 + 16]
                tile = i * rows // 8 + t
                mant[tile, :, cols] = jnp.where(keep, p, q).astype(BF16)
                mant[tile + 1, :, cols] = pltpu.roll(jnp.where(keep, q, p), turn, 0).astype(BF16)
        for t in range(i * rows // 8, (i + 1) * rows // 8):
            target = out_ref.at[block_of(core_ref[0], t // 8, t // 2 % 4, t % 2)]
            stores.append(pltpu.make_async_copy(mant.at[t], target, out_sem.at[t]))
            stores[t].start()
    for store in stores:
        store.wait()


def quantise(core, partials, other, amax, chunks=8):
    out = pl.pallas_call(
        quant_kernel,
        out_shape=jax.ShapeDtypeStruct((2, 2, 2, 2, 2, 8, HALF), BF16),
        in_specs=[SMEM, HBM, HBM, VMEM],
        out_specs=HBM,
        scratch_shapes=[
            pltpu.VMEM((ROWS, HALF), BF16),
            pltpu.VMEM((ROWS, HALF), BF16),
            pltpu.VMEM((ROWS // 8, 8, HALF), BF16),
            pltpu.SemaphoreType.DMA((chunks,)),
            pltpu.SemaphoreType.DMA((chunks,)),
            pltpu.SemaphoreType.DMA((ROWS // 8,)),
        ],
        compiler_params=PARAMS,
        name="quantise",
    )(core, partials, other, amax)
    return out.reshape(8, 32, HALF)


def rows_kernel(core_ref, w_ref, *refs):
    out_ref, full, out_sem = refs[-3:]
    half = pl.ds(pl.multiple_of(core_ref[0] * HALF, HALF), HALF)
    keep = rows_below(8 - 4 * core_ref[0])
    chunks = [(i >> 2, i >> 1 & 1, i & 1) for i in range(8)]
    stores = []
    for i, (ox, oz, jx) in enumerate(chunks):
        for jz in (0, 1):
            n = 2 * i + jz
            for b in range(NB):
                cols = slice(b * BLOCK, (b + 1) * BLOCK)
                p = w_ref[ox, oz, 0, jx, jz, :, cols].astype(F32)
                q = pltpu.roll(w_ref[ox, oz, 1, jx, jz, :, cols].astype(F32), 4, 0)
                full[n, :8, cols] = jnp.where(keep, p, q).astype(BF16)
                full[n, 8:, cols] = jnp.where(keep, q, p).astype(BF16)
            x = pick(1 - core_ref[0], ARRIVE, 2 * ox + jx)
            z = pick(core_ref[0], ARRIVE, 2 * oz + jz)
            at = pl.ds(pl.multiple_of(x * 64 + z * 16, 16), 16)
            stores.append(pltpu.make_async_copy(full.at[n], out_ref.at[at, half], out_sem.at[n]))
            stores[n].start()
    for store in stores:
        store.wait()


def place_rows(core, w, before=None):
    more = () if before is None else (before,)
    return pl.pallas_call(
        rows_kernel,
        out_shape=jax.ShapeDtypeStruct((ROWS, W), BF16),
        in_specs=[SMEM, VMEM, *(HBM for _ in more)],
        out_specs=HBM,
        scratch_shapes=[
            pltpu.VMEM((16, 16, HALF), BF16),
            pltpu.SemaphoreType.DMA((16,)),
        ],
        input_output_aliases={2: 0} if more else {},
        compiler_params=pltpu.CompilerParams(vmem_limit_bytes=24 << 20),
        name="place_rows",
    )(core, w.reshape(2, 2, 2, 2, 2, 8, HALF), *more)


def per_device(partials, master, moment_one, moment_two):
    d = lax.axis_index("dp")
    core, chip = d & 1, d >> 1
    first = core == 0
    row = chip * 4
    mine, theirs = core.reshape(1), (1 - core).reshape(1)

    amax, send = block_max(mine, partials)
    other = lax.ppermute(send, "dp", SWAP)
    amax = jnp.max(exchange(amax, Y_CORES), axis=0)
    amax = jnp.max(spread(amax, X_Z), axis=0)

    state = jnp.stack([master, moment_one, moment_two])
    state_own = lax.dynamic_slice_in_dim(state, core * HALF, HALF, 2)
    state_other = lax.dynamic_slice_in_dim(state, (1 - core) * HALF, HALF, 2)
    state_other = lax.ppermute(state_other, "dp", SWAP)
    state = jnp.where(
        first,
        jnp.concatenate([state_own, state_other], axis=1),
        jnp.concatenate([state_other, state_own], axis=1),
    )
    master, moment_one, moment_two = state

    mant = exchange(quantise(mine, partials, other, amax), NEAR_GROUPS)
    mant = jnp.sum(mant.astype(F32), axis=0).astype(F16).reshape(8, 4, HALF)
    total = jnp.sum(exchange(mant, FAR_GROUPS).astype(F32), axis=0)

    own_amax = lax.dynamic_slice(amax, (row & 127, (row >> 7) * NB), (4, NB))
    scale = scale_of(own_amax.astype(F32))
    factor = scale / (2.0**MBITS * N_DP)
    reduced_grad = (total.reshape(4, NB, BLOCK) * factor[:, :, None]).reshape(4, HALF)
    moment_one_new = 0.9 * moment_one + 0.1 * reduced_grad
    moment_two_new = 0.95 * moment_two + 0.05 * reduced_grad * reduced_grad
    update = (moment_one_new / (1.0 - 0.9**STEP)) / (
        jnp.sqrt(moment_two_new / (1.0 - 0.95**STEP)) + 1e-08
    )
    master_new = master - 0.001 * (update + 0.1 * master)
    blocks = master_new.reshape(4, NB, BLOCK)
    wscale = jnp.max(jnp.abs(blocks), axis=2) + 1e-06
    wmant = (blocks / wscale[:, :, None]).astype(BF16)
    weights = (wmant.astype(F32) * wscale[:, :, None]).reshape(4, HALF).astype(BF16)

    out = jnp.stack([master_new, moment_one_new, moment_two_new, reduced_grad])
    out_own = jnp.where(first, out[:, :2], out[:, 2:])
    out_other = lax.ppermute(jnp.where(first, out[:, 2:], out[:, :2]), "dp", SWAP)
    out = jnp.where(
        first,
        jnp.concatenate([out_own, out_other], axis=2),
        jnp.concatenate([out_other, out_own], axis=2),
    )

    weights = spread(weights, NEAR_GROUPS).reshape(32, HALF)
    weights = spread(weights, BACK_GROUPS)
    weights_other = lax.ppermute(weights, "dp", SWAP)
    full = place_rows(mine, weights)
    full = place_rows(theirs, weights_other, full)
    return (out[0], out[1], out[2], out[3], full)


def solution(mesh):
    in_specs = (P("dp", None, None), P("dp", None), P("dp", None), P("dp", None))
    out_specs = (P("dp", None), P("dp", None), P("dp", None), P("dp", None), P())
    return jax.shard_map(
        per_device, mesh=mesh, in_specs=in_specs, out_specs=out_specs, check_vma=False
    )
```
